32 devices in a mesh: pipe: 4 (over z), dp: 4 (over x, core), expert: 2 (over y).
Axes of the slice: x: 2, y: 2, z: 4, core: 2. Of those that a mesh axis runs over, the one named last changes fastest.
Arguments:
- block_input: bfloat16 [4, 1024, 3072], P('pipe', ('dp', 'expert')), may hold values from -6 to 6
- output_grad: bfloat16 [4, 1024, 3072], P('pipe', ('dp', 'expert')), may hold values from -6 to 6
- expert_ids: int32 [4, 1024, 6], P('pipe', ('dp', 'expert')), may hold values from 0 to 159, all different within a row
- gate_weights: float32 [4, 1024, 6], P('pipe', ('dp', 'expert')), may hold values from 0.25 to 2
- gate_proj: bfloat16 [4, 2, 3072, 1024], P('pipe', 'expert', None, 'dp'), may hold values from -0.109375 to 0.109375
- up_proj: bfloat16 [4, 2, 3072, 1024], P('pipe', 'expert', None, 'dp'), may hold values from -0.109375 to 0.109375
- down_proj: bfloat16 [4, 2, 1024, 3072], P('pipe', 'expert', 'dp'), may hold values from -0.1875 to 0.1875
Outputs:
- received_grad: bfloat16 [4, 1024, 3072], P('pipe', ('dp', 'expert'))
- gate_weight_grad: float32 [4, 1024, 6], P('pipe', ('dp', 'expert'))
- gate_proj_grad: bfloat16 [4, 2, 3072, 1024], P('pipe', 'expert', None, 'dp')
- up_proj_grad: bfloat16 [4, 2, 3072, 1024], P('pipe', 'expert', None, 'dp')
- down_proj_grad: bfloat16 [4, 2, 1024, 3072], P('pipe', 'expert', 'dp')
The draws below stay inside these ranges and needn't reach their ends.
Inputs may be any that keep to these rules, and one draw needn't show every extreme that they name: `expert_ids`: each token names 6 different experts.
All inputs are finite; a program needn't handle non-finite values.
Results may differ from the reference program's by a relative error of at most 0.006.
Values may be sent and summed in bfloat16 or wider, within the bound.
No kernel may reach another device: no remote copies, remote signals or barrier semaphores. Data moves between devices by JAX's collectives and lax.ppermute only.
A program may use at most 128 MiB of HBM per device.

```python
import math
import jax
import jax.numpy as jnp
from jax import lax

D = 3072
H = 1024
ROUTED = 160
TOP = 6
TOK_DEV = 128
SECTIONS = 4
EXPERTS = 2
CAP = 8
TOKENS = 1024


def shard_levels(stream_key, extent, shards, low, largest):
    def one(dim, blocks):
        heights = jax.random.uniform(jax.random.fold_in(jax.random.fold_in(stream_key, 6), dim), (blocks,), jnp.float32, low / len(shards), largest / len(shards))
        return jnp.repeat(jnp.exp(heights), extent[dim] // blocks).reshape((-1,) + (1,) * (len(extent) - dim - 1))

    level = one(*shards[0])
    for cut in shards[1:]:
        level = level * one(*cut)
    return level


def picks_of(key, rows, amount, top, lift):
    sequence = jax.random.permutation(jax.random.fold_in(key, 1), amount)
    favour = sequence
    for power in range(3):
        favour = favour * favour // amount
    favour = favour * lift // amount
    tickets = jax.random.randint(jax.random.fold_in(key, 2), (rows, amount), 0, 4096) + favour
    sure = jax.random.permutation(jax.random.fold_in(key, 3), rows)[jnp.arange(amount) % rows]
    tickets = jnp.where(jnp.arange(rows)[:, None] == sure[None, :], 1 << 14, tickets)
    merit = tickets * amount + jnp.arange(amount)
    return lax.top_k(merit.astype(jnp.int32), top)[1].astype(jnp.int32)


def noise(stream_key, extent, deviation, limit, shards=(), kind=jnp.bfloat16):
    result = deviation * jax.random.normal(stream_key, extent, jnp.float32)
    if shards:
        result = result * shard_levels(stream_key, extent, shards, -0.22, 0.18)
    return jnp.clip(result, -limit, limit).astype(kind)


def setup_inputs(seed: int = 0) -> dict:
    key_list = jax.random.split(jax.random.key(seed), 8)
    return {
        "block_input": noise(key_list[0], (SECTIONS, TOKENS, D), 1.0, 6.0, ((0, 4), (1, 8))),
        "output_grad": noise(key_list[1], (SECTIONS, TOKENS, D), 1.0, 6.0, ((0, 4), (1, 8))),
        "expert_ids": picks_of(key_list[2], SECTIONS * TOKENS, ROUTED, TOP, 614).reshape((SECTIONS, TOKENS, TOP)),
        "gate_weights": jnp.clip(jnp.exp(math.log(2.0) - 2.0794415 * jax.random.uniform(key_list[3], (SECTIONS, TOKENS, TOP), jnp.float32) ** shard_levels(key_list[3], (SECTIONS, TOKENS, TOP), ((0, 4), (1, 8)), -0.2, 0.2)), 0.25, 2.0),
        "gate_proj": noise(key_list[4], (SECTIONS, EXPERTS, D, H), D ** -0.5, 0.109375, ((0, 4), (1, 2), (3, 4))),
        "up_proj": noise(key_list[5], (SECTIONS, EXPERTS, D, H), D ** -0.5, 0.109375, ((0, 4), (1, 2), (3, 4))),
        "down_proj": noise(key_list[6], (SECTIONS, EXPERTS, H, D), H ** -0.5, 0.1875, ((0, 4), (1, 2), (2, 4))),
    }


def section_backward(acts, grads, chosen_ids, weights, gate_w, up_w, down_w):
    blocks = TOKENS // TOK_DEV
    pairs = TOK_DEV * TOP
    block_ids = chosen_ids.reshape(blocks, pairs)
    columns = jnp.arange(EXPERTS, dtype=jnp.int32)
    onehot = (block_ids[:, :, None] == columns[None, None, :]).astype(jnp.int32)
    earlier = jnp.cumsum(onehot, axis=1) - onehot
    slot_rank = jnp.sum(earlier * onehot, axis=2)
    kept = (block_ids < EXPERTS) & (slot_rank < CAP)
    block_pos = jnp.arange(blocks, dtype=jnp.int32)[:, None]
    total = EXPERTS * blocks * CAP
    slot_index = jnp.where(kept, block_ids * (blocks * CAP) + block_pos * CAP + slot_rank, total).reshape(-1).astype(jnp.int32)
    pair_token = (jnp.arange(TOKENS * TOP, dtype=jnp.int32) // TOP).astype(jnp.int32)
    source_token = jnp.zeros((total + 1,), jnp.int32).at[slot_index].set(pair_token)[:total]
    slot_weight = jnp.zeros((total + 1,), weights.dtype).at[slot_index].set(weights.reshape(-1))[:total]
    filled = jnp.zeros((total + 1,), jnp.bool_).at[slot_index].set(True)[:total]
    disp_acts = jnp.where(filled[:, None], acts[source_token], jnp.zeros((), acts.dtype)).astype(acts.dtype)
    scaled = slot_weight[:, None] * grads[source_token].astype(jnp.float32)
    disp_grad = jnp.where(filled[:, None], scaled, jnp.zeros((), scaled.dtype)).astype(jnp.bfloat16)
    disp_acts = disp_acts.reshape(EXPERTS, blocks * CAP, D)
    disp_grad = disp_grad.reshape(EXPERTS, blocks * CAP, D)

    def expert_pass(items):
        rows_in, rows_grad, w_gate, w_upper, w_lower = items
        gate_pre = jnp.dot(rows_in, w_gate, preferred_element_type=jnp.float32)
        up_value = jnp.dot(rows_in, w_upper, preferred_element_type=jnp.float32)
        grad_hidden = jnp.dot(rows_grad, w_lower.T, preferred_element_type=jnp.float32)
        sigma_gate = jax.nn.sigmoid(gate_pre)
        swish = gate_pre * sigma_gate
        hidden = swish * up_value
        scores = jnp.sum(hidden * grad_hidden, axis=1)
        lower_grad = jnp.dot(hidden.astype(jnp.bfloat16).T, rows_grad, preferred_element_type=jnp.float32).astype(jnp.bfloat16)
        delta_gate = (grad_hidden * up_value * sigma_gate * (1.0 + gate_pre * (1.0 - sigma_gate))).astype(jnp.bfloat16)
        delta_up = (grad_hidden * swish).astype(jnp.bfloat16)
        gate_grad = jnp.dot(rows_in.T, delta_gate, preferred_element_type=jnp.float32).astype(jnp.bfloat16)
        upper_grad = jnp.dot(rows_in.T, delta_up, preferred_element_type=jnp.float32).astype(jnp.bfloat16)
        slot_grad = (jnp.dot(delta_gate, w_gate.T, preferred_element_type=jnp.float32)
                     + jnp.dot(delta_up, w_upper.T, preferred_element_type=jnp.float32)).astype(jnp.bfloat16)
        return gate_grad, upper_grad, lower_grad, slot_grad, scores

    results = lax.map(expert_pass, (disp_acts, disp_grad, gate_w, up_w, down_w))
    slot_grad = results[3].reshape(total, D).astype(jnp.float32)
    slot_grad = jnp.where(filled[:, None], slot_grad, jnp.zeros((), slot_grad.dtype))
    input_grad = jax.ops.segment_sum(slot_grad, source_token, num_segments=TOKENS).astype(jnp.bfloat16)
    scores = jnp.concatenate([results[4].reshape(total), jnp.zeros((1,), results[4].dtype)])
    weight_grad = (scores[slot_index] / weights.reshape(-1)).reshape(TOKENS, TOP)
    return input_grad, weight_grad, results[0], results[1], results[2]


def reference(block_input, output_grad, expert_ids, gate_weights, gate_proj, up_proj, down_proj):
    outputs = [section_backward(block_input[s], output_grad[s], expert_ids[s], gate_weights[s],
                              gate_proj[s], up_proj[s], down_proj[s]) for s in range(SECTIONS)]
    input_grads = jnp.stack([item[0] for item in outputs])
    received_grad = jnp.roll(input_grads, -1, axis=0)
    weight_grad = jnp.stack([item[1] for item in outputs])
    gate_grads = jnp.stack([item[2] for item in outputs])
    upper_grads = jnp.stack([item[3] for item in outputs])
    lower_grads = jnp.stack([item[4] for item in outputs])
    return (received_grad, weight_grad, gate_grads, upper_grads, lower_grads)
```

```python
import functools

import jax
import jax.numpy as jnp
from jax import lax
from jax.experimental import pallas as pl
from jax.experimental.pallas import tpu as pltpu
from jax.sharding import PartitionSpec as P

PAIRWISE_MAX = 8
LANES = 128
VMEM = pl.BlockSpec(memory_space=pltpu.VMEM)
ANY = pl.BlockSpec(memory_space=pl.ANY)


def shape_of(shape, dtype):
    return jax.ShapeDtypeStruct(shape, dtype)


def cost(flops, bytes_moved):
    return pl.CostEstimate(flops=flops, bytes_accessed=bytes_moved, transcendentals=0)


def power_of_two(number):
    return number > 0 and number & (number - 1) == 0


def swap(value, offset):
    count = lax.axis_size("dp") * lax.axis_size("expert")
    return lax.ppermute(value, ("dp", "expert"), [(i, i ^ offset) for i in range(count)])


def swap_back(value, offset):
    sections = lax.axis_size("pipe")
    count = lax.axis_size("dp") * lax.axis_size("expert")
    pairs = [
        (s * count + i, ((s - 1) % sections) * count + (i ^ offset))
        for s in range(sections)
        for i in range(count)
    ]
    return lax.ppermute(value, ("pipe", "dp", "expert"), pairs)


def pick_kernel(capacity, groups, own_ref, ids_ref, weight_ref, acts_ref, grad_ref, *refs):
    outs = refs[:groups]
    select_ref, acts_buf, grad_buf, sems = refs[groups:]
    acts_copy = pltpu.make_async_copy(acts_ref, acts_buf, sems.at[0])
    grad_copy = pltpu.make_async_copy(grad_ref, grad_buf, sems.at[1])
    acts_copy.start()
    grad_copy.start()
    chosen, _, tokens = ids_ref.shape
    rows = groups * capacity
    row = lax.broadcasted_iota(jnp.int32, (rows, tokens), 0)
    row_expert = (row // capacity) ^ own_ref[0]
    taken = jnp.zeros((rows, tokens), jnp.float32)
    scale = jnp.zeros((rows, tokens), jnp.float32)
    for k in range(chosen):
        same = ids_ref[k] == row_expert
        taken = jnp.where(same, 1.0, taken)
        scale = jnp.where(same, weight_ref[k], scale)
    before = lax.broadcasted_iota(jnp.int32, (tokens, tokens), 0)
    after = lax.broadcasted_iota(jnp.int32, (tokens, tokens), 1)
    earlier = jnp.where(before < after, 1.0, 0.0).astype(jnp.bfloat16)
    rank = jnp.dot(taken.astype(jnp.bfloat16), earlier, preferred_element_type=jnp.float32)
    slot = (row % capacity).astype(jnp.float32)
    select = jnp.where(rank == slot, taken, 0.0)
    row_scale = jnp.sum(select * scale, axis=1, keepdims=True)
    select = select.astype(jnp.bfloat16)
    select_ref[...] = select
    acts_copy.wait()
    acts_rows = jnp.dot(select, acts_buf[...], preferred_element_type=jnp.float32)
    grad_copy.wait()
    grad_rows = jnp.dot(select, grad_buf[...], preferred_element_type=jnp.float32) * row_scale
    for j in range(groups):
        part = slice(j * capacity, (j + 1) * capacity)
        outs[j][...] = jnp.concatenate([acts_rows[part], grad_rows[part]], axis=0).astype(jnp.bfloat16)


def pick_rows(own, ids, weights, acts, grads, groups, capacity):
    tokens, width = acts.shape
    group = shape_of((2 * capacity, width), jnp.bfloat16)
    return pl.pallas_call(
        functools.partial(pick_kernel, capacity, groups),
        out_shape=[group] * groups + [shape_of((groups * capacity, tokens), jnp.bfloat16)],
        in_specs=[pl.BlockSpec(memory_space=pltpu.SMEM), VMEM, VMEM, ANY, ANY],
        out_specs=[VMEM] * (groups + 1),
        scratch_shapes=[
            pltpu.VMEM((tokens, width), jnp.bfloat16),
            pltpu.VMEM((tokens, width), jnp.bfloat16),
            pltpu.SemaphoreType.DMA((2,)),
        ],
        cost_estimate=cost(4 * groups * capacity * tokens * width, 4 * tokens * width),
        compiler_params=pltpu.CompilerParams(vmem_limit_bytes=16 * 2**20),
        name="pick_rows",
    )(own, ids, weights, acts, grads)


def split_rows(value, capacity):
    pieces = value.shape[0] // (2 * capacity)
    upper = [value[2 * p * capacity : (2 * p + 1) * capacity] for p in range(pieces)]
    lower = [value[(2 * p + 1) * capacity : (2 * p + 2) * capacity] for p in range(pieces)]
    return jnp.concatenate(upper, axis=0), jnp.concatenate(lower, axis=0)


def weave(value, capacity, upper):
    blank = jnp.zeros((capacity, value.shape[1]), value.dtype)
    parts = []
    for p in range(value.shape[0] // capacity):
        part = value[p * capacity : (p + 1) * capacity]
        parts += [part, blank] if upper else [blank, part]
    return jnp.concatenate(parts, axis=0)


def hidden_kernel(capacity, pieces, *refs):
    piece_refs = refs[:pieces]
    gate_ref, upper_ref, lower_ref = refs[pieces : pieces + 3]
    keep_ref, send_ref, score_ref, delta_ref, hidden_ref = refs[pieces + 3 :]
    rows = jnp.concatenate([ref[...] for ref in piece_refs], axis=0)
    across = (((1,), (1,)), ((), ()))
    gate_pre, _ = split_rows(jnp.dot(rows, gate_ref[...], preferred_element_type=jnp.float32), capacity)
    up_value, _ = split_rows(jnp.dot(rows, upper_ref[...], preferred_element_type=jnp.float32), capacity)
    _, grad_hidden = split_rows(
        lax.dot_general(rows, lower_ref[...], across, preferred_element_type=jnp.float32), capacity
    )
    sigma_gate = jax.nn.sigmoid(gate_pre)
    swish = gate_pre * sigma_gate
    hidden = swish * up_value
    scores = jnp.sum(hidden * grad_hidden, axis=1, keepdims=True)
    delta_gate = grad_hidden * up_value * sigma_gate * (1.0 + gate_pre * (1.0 - sigma_gate))
    delta_up = grad_hidden * swish
    partial_rows = lax.dot_general(
        delta_gate.astype(jnp.bfloat16), gate_ref[...], across, preferred_element_type=jnp.float32
    ) + lax.dot_general(
        delta_up.astype(jnp.bfloat16), upper_ref[...], across, preferred_element_type=jnp.float32
    )
    half, width = keep_ref.shape
    units = gate_ref.shape[1]
    keep_ref[...] = partial_rows[:half]
    send_ref[:, :width] = partial_rows[half:].astype(jnp.bfloat16)
    score_ref[...] = jnp.broadcast_to(scores[:half], (half, LANES))
    rest = scores[half:]
    high = rest.astype(jnp.bfloat16).astype(jnp.float32)
    middle = (rest - high).astype(jnp.bfloat16).astype(jnp.float32)
    low = rest - high - middle
    lane = lax.broadcasted_iota(jnp.int32, (half, LANES), 1)
    parts = jnp.where(lane == 0, high, jnp.where(lane == 1, middle, jnp.where(lane == 2, low, 0.0)))
    send_ref[:, width:] = parts.astype(jnp.bfloat16)
    delta_ref[:, :units] = weave(delta_gate, capacity, True).astype(jnp.bfloat16)
    delta_ref[:, units:] = weave(delta_up, capacity, True).astype(jnp.bfloat16)
    hidden_ref[...] = weave(hidden, capacity, False).astype(jnp.bfloat16)


def hidden_pass(pieces, gate, upper, lower, capacity):
    width, units = gate.shape
    count = len(pieces)
    half = count * capacity // 2
    rows = 2 * count * capacity
    return pl.pallas_call(
        functools.partial(hidden_kernel, capacity, count),
        out_shape=[
            shape_of((half, width), jnp.float32),
            shape_of((half, width + LANES), jnp.bfloat16),
            shape_of((half, LANES), jnp.float32),
            shape_of((rows, 2 * units), jnp.bfloat16),
            shape_of((rows, units), jnp.bfloat16),
        ],
        in_specs=[VMEM] * (count + 3),
        out_specs=[VMEM] * 5,
        cost_estimate=cost(10 * rows * width * units, 6 * width * units),
        compiler_params=pltpu.CompilerParams(vmem_limit_bytes=24 * 2**20),
        name="hidden_pass",
    )(*pieces, gate, upper, lower)


def join_kernel(capacity, groups, keep_ref, score_ref, recv_ref, *out_refs):
    width = keep_ref.shape[1]
    for j in range(groups):
        part = slice(j * capacity, (j + 1) * capacity)
        other = recv_ref[part, :width].astype(jnp.float32)
        out_refs[j][...] = (keep_ref[part] + other).astype(jnp.bfloat16)
    extra = recv_ref[:, width:].astype(jnp.float32)
    out_refs[groups][...] = score_ref[...] + jnp.sum(extra, axis=1, keepdims=True)


def join_cores(keep, scores, recv, groups, capacity):
    half, width = keep.shape
    return pl.pallas_call(
        functools.partial(join_kernel, capacity, groups),
        out_shape=[shape_of((capacity, width), jnp.bfloat16)] * groups + [shape_of((half, LANES), jnp.float32)],
        in_specs=[VMEM] * 3,
        out_specs=[VMEM] * (groups + 1),
        cost_estimate=cost(2 * half * width, 8 * half * width),
        compiler_params=pltpu.CompilerParams(vmem_limit_bytes=8 * 2**20),
        name="join_cores",
    )(keep, scores, recv)


def weights_kernel(pieces, step, *refs):
    piece_refs = refs[:pieces]
    delta_ref, hidden_ref, gate_out, upper_out, lower_out = refs[pieces:]
    start = pl.multiple_of(pl.program_id(0) * step, step)
    rows = jnp.concatenate([ref[:, pl.ds(start, step)] for ref in piece_refs], axis=0)
    down = (((0,), (0,)), ((), ()))
    both = lax.dot_general(rows, delta_ref[...], down, preferred_element_type=jnp.float32)
    units = gate_out.shape[1]
    gate_out[...] = both[:, :units].astype(jnp.bfloat16)
    upper_out[...] = both[:, units:].astype(jnp.bfloat16)
    lower_out[...] = lax.dot_general(
        hidden_ref[...], rows, down, preferred_element_type=jnp.float32
    ).astype(jnp.bfloat16)


def weight_grads(pieces, delta, hidden, step):
    width = pieces[0].shape[1]
    rows, units = hidden.shape
    count = len(pieces)

    def whole(array):
        return pl.BlockSpec(array.shape, lambda i: (0, 0))

    return pl.pallas_call(
        functools.partial(weights_kernel, count, step),
        grid=(width // step,),
        out_shape=[
            shape_of((width, units), jnp.bfloat16),
            shape_of((width, units), jnp.bfloat16),
            shape_of((units, width), jnp.bfloat16),
        ],
        in_specs=[whole(array) for array in (*pieces, delta, hidden)],
        out_specs=[
            pl.BlockSpec((step, units), lambda i: (i, 0)),
            pl.BlockSpec((step, units), lambda i: (i, 0)),
            pl.BlockSpec((units, step), lambda i: (0, i)),
        ],
        cost_estimate=cost(6 * rows * width * units, 6 * width * units),
        compiler_params=pltpu.CompilerParams(vmem_limit_bytes=24 * 2**20),
        name="weight_grads",
    )(*pieces, delta, hidden)


def score_kernel(capacity, groups, own_ref, ids_ref, weight_ref, select_ref, *refs):
    out_ref = refs[-1]
    chosen, _, tokens = ids_ref.shape
    sums = []
    for j in range(groups):
        part = slice(j * capacity, (j + 1) * capacity)
        picked = select_ref[part].astype(jnp.float32) * refs[j][:, :1]
        sums.append(jnp.sum(picked, axis=0, keepdims=True))
    for k in range(chosen):
        value = jnp.zeros((1, tokens), jnp.float32)
        for j in range(groups):
            value = jnp.where(ids_ref[k] == (own_ref[0] ^ j), sums[j], value)
        out_ref[k] = value / weight_ref[k]


def score_grads(own, ids, weights, select, scores, capacity):
    groups = len(scores)
    return pl.pallas_call(
        functools.partial(score_kernel, capacity, groups),
        out_shape=shape_of(weights.shape, jnp.float32),
        in_specs=[pl.BlockSpec(memory_space=pltpu.SMEM)] + [VMEM] * (3 + groups),
        out_specs=VMEM,
        cost_estimate=cost(1000, 1000),
        compiler_params=pltpu.CompilerParams(vmem_limit_bytes=4 * 2**20),
        name="score_grads",
    )(own, ids, weights, select, *scores)


def spread_kernel(groups, terms, select_ref, *refs):
    out_ref = refs[-1]
    sums = []
    for j in range(groups):
        total = refs[j * terms][...].astype(jnp.float32)
        for term in range(1, terms):
            total = total + refs[j * terms + term][...].astype(jnp.float32)
        sums.append(total)
    slot_grad = jnp.concatenate(sums, axis=0).astype(jnp.bfloat16)
    out_ref[...] = lax.dot_general(
        select_ref[...], slot_grad, (((0,), (0,)), ((), ())), preferred_element_type=jnp.float32
    ).astype(jnp.bfloat16)


def spread_rows(select, groups, step):
    tokens = select.shape[1]
    capacity, width = groups[0][0].shape
    terms = len(groups[0])
    flat = [array for group in groups for array in group]
    return pl.pallas_call(
        functools.partial(spread_kernel, len(groups), terms),
        grid=(width // step,),
        out_shape=shape_of((tokens, width), jnp.bfloat16),
        in_specs=[pl.BlockSpec(select.shape, lambda i: (0, 0))]
        + [pl.BlockSpec((capacity, step), lambda i: (0, i)) for _ in flat],
        out_specs=pl.BlockSpec((tokens, step), lambda i: (0, i)),
        cost_estimate=cost(2 * select.shape[0] * tokens * width, 2 * tokens * width),
        compiler_params=pltpu.CompilerParams(vmem_limit_bytes=16 * 2**20),
        name="spread_rows",
    )(select, *flat)


def pairwise_shards(block_input, output_grad, expert_ids, gate_weights, gate_proj, up_proj, down_proj):
    tokens = block_input.shape[1]
    width = block_input.shape[2]
    capacity = tokens // 16
    groups = lax.axis_size("expert")
    partner = groups
    count = lax.axis_size("dp") * groups
    plane = [offset for offset in range(count) if not offset & partner]
    own = lax.axis_index("expert").astype(jnp.int32).reshape(1)
    ids = jnp.transpose(expert_ids, (2, 0, 1))
    weights = jnp.transpose(gate_weights, (2, 0, 1))
    *sends, select = pick_rows(own, ids, weights, block_input[0], output_grad[0], groups, capacity)
    select_next = swap_back(select, 0)
    mine = {0: sends[0]}
    for offset in sorted(plane[1:], reverse=True):
        mine[offset] = swap(sends[offset % groups], offset)
    theirs = {offset: swap(mine[offset], partner) for offset in plane}
    pieces = [mine[offset] for offset in plane] + [theirs[offset] for offset in plane]
    keep, send, scores, delta, hidden = hidden_pass(
        pieces, gate_proj[0, 0], up_proj[0, 0], down_proj[0, 0], capacity
    )
    recv = swap(send, partner)
    *joined, scores = join_cores(keep, scores, recv, len(plane), capacity)
    back = {offset: swap_back(joined[i], offset) for i, offset in enumerate(plane)}
    gate_grad, upper_grad, lower_grad = weight_grads(pieces, delta, hidden, 512)
    score_rows = {offset: scores[i * capacity : (i + 1) * capacity, :] for i, offset in enumerate(plane)}
    bit = count // 2
    while bit > partner:
        low = [offset for offset in score_rows if not offset & bit]
        moved = swap(jnp.concatenate([score_rows[offset | bit][:, :1] for offset in low]), bit)
        score_rows = {
            offset: score_rows[offset][:, :1] + moved[i * capacity : (i + 1) * capacity]
            for i, offset in enumerate(low)
        }
        bit //= 2
    score_list = [
        score_rows[j][:, :1] if j == 0 else swap(score_rows[j][:, :1], j) for j in range(groups)
    ]
    weight_grad = score_grads(own, ids, weights, select, score_list, capacity)
    received = spread_rows(
        select_next,
        [[back[offset] for offset in plane if offset % groups == j] for j in range(groups)],
        width // 2,
    )
    return (
        received[None],
        jnp.transpose(weight_grad, (1, 2, 0)),
        gate_grad[None, None],
        upper_grad[None, None],
        lower_grad[None, None],
    )


def shifted(value, axis, steps):
    count = lax.axis_size(axis)
    pairs = [(source, (source + steps) % count) for source in range(count)]
    return lax.ppermute(value, axis, pairs)


def slot_tables(chosen_ids, experts, capacity):
    tok_count, chosen = chosen_ids.shape
    flat_ids = chosen_ids.reshape(-1)
    columns = jnp.arange(experts, dtype=jnp.int32)
    onehot = (flat_ids[:, None] == columns[None, :]).astype(jnp.int32)
    earlier = jnp.cumsum(onehot, axis=0) - onehot
    slot_rank = jnp.sum(earlier * onehot, axis=1)
    kept_pair = (flat_ids < experts) & (slot_rank < capacity)
    slot_index = jnp.where(kept_pair, flat_ids * capacity + slot_rank, experts * capacity)
    slot_rows = jnp.arange(experts * capacity, dtype=jnp.int32)
    placed = slot_index[None, :] == slot_rows[:, None]
    pair_index = jnp.arange(tok_count * chosen, dtype=jnp.int32)
    source_pair = jnp.sum(jnp.where(placed, pair_index[None, :], 0), axis=1)
    filled = jnp.any(placed, axis=1)
    return (slot_index, source_pair, filled)


def general_shards(block_input, output_grad, expert_ids, gate_weights, gate_proj, up_proj, down_proj):
    acts_local = block_input[0]
    grad_local = output_grad[0]
    chosen_ids = expert_ids[0]
    route_weight = gate_weights[0]
    tok_count, chosen = chosen_ids.shape
    width = acts_local.shape[1]
    local_count = gate_proj.shape[1]
    dp_count = lax.axis_size("dp")
    expert_count = lax.axis_size("expert")
    experts = local_count * expert_count
    capacity = tok_count // 16
    slot_index, source_pair, filled = slot_tables(chosen_ids, experts, capacity)
    source_token = source_pair // chosen
    slot_weight = route_weight.reshape(-1)[source_pair]
    send_acts = jnp.where(filled[:, None], acts_local[source_token], jnp.zeros((), jnp.bfloat16))
    scaled = slot_weight[:, None] * grad_local[source_token].astype(jnp.float32)
    send_grad = jnp.where(filled[:, None], scaled, 0.0).astype(jnp.bfloat16)
    send_acts = send_acts.reshape(experts, capacity, width)
    send_grad = send_grad.reshape(experts, capacity, width)
    acts_copies = jnp.broadcast_to(send_acts[None], (dp_count,) + send_acts.shape).reshape(
        dp_count * experts, capacity, width
    )
    grad_copies = jnp.broadcast_to(send_grad[None], (dp_count,) + send_grad.shape).reshape(
        dp_count * experts, capacity, width
    )
    recv_acts, recv_grad = (
        lax.all_to_all(acts_copies, ("dp", "expert"), split_axis=0, concat_axis=1, tiled=True),
        lax.all_to_all(grad_copies, ("dp", "expert"), split_axis=0, concat_axis=1, tiled=True),
    )
    gate_local = gate_proj[0]
    upper_local = up_proj[0]
    lower_local = down_proj[0]
    gate_pre = jnp.einsum("erd,edh->erh", recv_acts, gate_local, preferred_element_type=jnp.float32)
    up_value = jnp.einsum(
        "erd,edh->erh", recv_acts, upper_local, preferred_element_type=jnp.float32
    )
    grad_hidden = jnp.einsum(
        "erd,ehd->erh", recv_grad, lower_local, preferred_element_type=jnp.float32
    )
    sigma_gate = jax.nn.sigmoid(gate_pre)
    swish = gate_pre * sigma_gate
    hidden = swish * up_value
    scores = jnp.sum(hidden * grad_hidden, axis=2)
    lower_grad = jnp.einsum(
        "erh,erd->ehd", hidden.astype(jnp.bfloat16), recv_grad, preferred_element_type=jnp.float32
    ).astype(jnp.bfloat16)
    delta_gate = (
        grad_hidden * up_value * sigma_gate * (1.0 + gate_pre * (1.0 - sigma_gate))
    ).astype(jnp.bfloat16)
    delta_up = (grad_hidden * swish).astype(jnp.bfloat16)
    gate_grad = jnp.einsum(
        "erd,erh->edh", recv_acts, delta_gate, preferred_element_type=jnp.float32
    ).astype(jnp.bfloat16)
    upper_grad = jnp.einsum(
        "erd,erh->edh", recv_acts, delta_up, preferred_element_type=jnp.float32
    ).astype(jnp.bfloat16)
    partial_value = jnp.einsum(
        "erh,edh->erd", delta_gate, gate_local, preferred_element_type=jnp.float32
    ) + jnp.einsum("erh,edh->erd", delta_up, upper_local, preferred_element_type=jnp.float32)
    back_rows, back_scores = (
        lax.all_to_all(partial_value, ("dp", "expert"), split_axis=1, concat_axis=0, tiled=True),
        lax.all_to_all(scores, ("dp", "expert"), split_axis=1, concat_axis=0, tiled=True),
    )
    slot_grad = jnp.sum(back_rows.reshape(dp_count, experts * capacity, width), axis=0).astype(
        jnp.bfloat16
    )
    slot_scores = jnp.sum(back_scores.reshape(dp_count, experts * capacity), axis=0)
    token_rows = jnp.arange(tok_count, dtype=jnp.int32)
    token_map = ((source_token[:, None] == token_rows[None, :]) & filled[:, None]).astype(
        jnp.bfloat16
    )
    input_grad = jnp.einsum(
        "st,sd->td", token_map, slot_grad, preferred_element_type=jnp.float32
    ).astype(jnp.bfloat16)
    padded_scores = jnp.concatenate([slot_scores, jnp.zeros((1,), jnp.float32)])
    weight_grad = (padded_scores[slot_index] / route_weight.reshape(-1)).reshape(tok_count, chosen)
    received = shifted(input_grad, "pipe", -1)
    return (received[None], weight_grad[None], gate_grad[None], upper_grad[None], lower_grad[None])


def solution(mesh):
    in_specs = (
        P("pipe", ("dp", "expert"), None),
        P("pipe", ("dp", "expert"), None),
        P("pipe", ("dp", "expert"), None),
        P("pipe", ("dp", "expert"), None),
        P("pipe", "expert", None, "dp"),
        P("pipe", "expert", None, "dp"),
        P("pipe", "expert", "dp", None),
    )
    out_specs = (
        P("pipe", ("dp", "expert"), None),
        P("pipe", ("dp", "expert"), None),
        P("pipe", "expert", None, "dp"),
        P("pipe", "expert", None, "dp"),
        P("pipe", "expert", "dp", None),
    )
    dp_count, expert_count = mesh.shape["dp"], mesh.shape["expert"]

    def shards(*arrays):
        pairwise = (
            dp_count * expert_count <= PAIRWISE_MAX
            and dp_count > 1
            and power_of_two(dp_count)
            and power_of_two(expert_count)
            and arrays[4].shape[1] == 1
        )
        return (pairwise_shards if pairwise else general_shards)(*arrays)

    return jax.shard_map(shards, mesh=mesh, in_specs=in_specs, out_specs=out_specs, check_vma=False)
```

```python
import functools

import jax
import jax.numpy as jnp
from jax import lax
from jax.experimental import pallas as pl
from jax.experimental.pallas import tpu as pltpu
from jax.sharding import PartitionSpec as P


PAIRWISE_MAX = 8
LANES = 128
VMEM = pl.BlockSpec(memory_space=pltpu.VMEM)
HBM = pl.BlockSpec(memory_space=pltpu.HBM)


def shape_of(shape, dtype):
    return jax.ShapeDtypeStruct(shape, dtype)


def cost(flops, bytes_moved):
    return pl.CostEstimate(flops=flops, bytes_accessed=bytes_moved, transcendentals=0)


def power_of_two(number):
    return number > 0 and number & (number - 1) == 0


def swap(value, offset):
    count = lax.axis_size("dp") * lax.axis_size("expert")
    return lax.ppermute(value, ("dp", "expert"), [(i, i ^ offset) for i in range(count)])


def send_back(value, across):
    sections = lax.axis_size("pipe")
    chips = lax.axis_size("dp") // 2
    pairs = []
    for s in range(sections):
        for x in range(chips):
            for core in range(2):
                for expert in range(2):
                    source = (s * chips + x) * 4 + 2 * core + expert
                    target = (((s - 1) % sections) * chips + (x ^ across)) * 4 + 2 * expert + core
                    pairs.append((source, target))
    return lax.ppermute(value, ("pipe", "dp", "expert"), pairs)


def pick_kernel(capacity, own_ref, ids_hbm, weight_hbm, acts_hbm, grad_hbm, *refs):
    outs = refs[:2]
    select_ref, ids_ref, weight_ref, acts_ref, grad_ref, sems = refs[2:]
    copies = [
        pltpu.make_async_copy(source, target, sems.at[i])
        for i, (source, target) in enumerate(
            [(ids_hbm, ids_ref), (weight_hbm, weight_ref), (acts_hbm, acts_ref), (grad_hbm, grad_ref)]
        )
    ]
    for copy in copies:
        copy.start()
    chosen, _, tokens = ids_ref.shape
    width = acts_ref.shape[1]
    rows = 2 * capacity
    row = lax.broadcasted_iota(jnp.int32, (rows, tokens), 0)
    row_expert = (row // capacity) ^ own_ref[0]
    before = lax.broadcasted_iota(jnp.int32, (tokens, tokens), 0)
    after = lax.broadcasted_iota(jnp.int32, (tokens, tokens), 1)
    earlier = jnp.where(before < after, 1.0, 0.0).astype(jnp.bfloat16)
    slot = (row % capacity).astype(jnp.float32)
    token = lax.broadcasted_iota(jnp.int32, (rows, tokens), 1).astype(jnp.float32)
    lane = lax.broadcasted_iota(jnp.int32, (rows, LANES), 1)
    taken = jnp.zeros((rows, tokens), jnp.float32)
    scale = jnp.zeros((rows, tokens), jnp.float32)
    copies[0].wait()
    copies[1].wait()
    for k in range(chosen):
        same = ids_ref[k] == row_expert
        taken = jnp.where(same, 1.0, taken)
        scale = jnp.where(same, weight_ref[k], scale)
    rank = jnp.dot(taken.astype(jnp.bfloat16), earlier, preferred_element_type=jnp.float32)
    select = jnp.where(rank == slot, taken, 0.0)
    row_scale = jnp.sum(select * scale, axis=1, keepdims=True)
    number = jnp.sum(select * (token + 1.0), axis=1, keepdims=True)
    high = jnp.floor(number / 256.0)
    marks = jnp.where(lane == 0, high, jnp.where(lane == 1, number - 256.0 * high, 0.0))
    select = select.astype(jnp.bfloat16)
    select_ref[...] = select
    copies[2].wait()
    acts_rows = jnp.dot(select, acts_ref[...], preferred_element_type=jnp.float32)
    copies[3].wait()
    grad_rows = jnp.dot(select, grad_ref[...], preferred_element_type=jnp.float32) * row_scale
    for j in range(2):
        part = slice(j * capacity, (j + 1) * capacity)
        outs[j][:, :width] = jnp.concatenate([acts_rows[part], grad_rows[part]], axis=0).astype(jnp.bfloat16)
        outs[j][:, width:] = jnp.concatenate([marks[part]] * 2, axis=0).astype(jnp.bfloat16)


def pick_rows(own, ids, weights, acts, grads, capacity):
    tokens, width = acts.shape
    group = shape_of((2 * capacity, width + LANES), jnp.bfloat16)
    return pl.pallas_call(
        functools.partial(pick_kernel, capacity),
        out_shape=[group, group, shape_of((2 * capacity, tokens), jnp.bfloat16)],
        in_specs=[pl.BlockSpec(memory_space=pltpu.SMEM)] + [HBM] * 4,
        out_specs=[VMEM] * 3,
        scratch_shapes=[
            pltpu.VMEM(ids.shape, jnp.int32),
            pltpu.VMEM(weights.shape, jnp.float32),
            pltpu.VMEM((tokens, width), jnp.bfloat16),
            pltpu.VMEM((tokens, width), jnp.bfloat16),
            pltpu.SemaphoreType.DMA((4,)),
        ],
        cost_estimate=cost(8 * capacity * tokens * width, 4 * tokens * width),
        compiler_params=pltpu.CompilerParams(vmem_limit_bytes=16 * 2**20),
        name="pick_rows",
    )(own, ids, weights, acts, grads)


def load_kernel(gate_hbm, upper_hbm, gate_ref, upper_ref, sems):
    gate_copy = pltpu.make_async_copy(gate_hbm, gate_ref, sems.at[0])
    upper_copy = pltpu.make_async_copy(upper_hbm.at[: upper_ref.shape[0]], upper_ref, sems.at[1])
    gate_copy.start()
    upper_copy.start()
    gate_copy.wait()
    upper_copy.wait()


def load_weights(gate, upper):
    width, units = gate.shape
    return pl.pallas_call(
        load_kernel,
        out_shape=[shape_of((width, units), gate.dtype), shape_of((width // 2, units), upper.dtype)],
        in_specs=[HBM] * 2,
        out_specs=[VMEM] * 2,
        scratch_shapes=[pltpu.SemaphoreType.DMA((2,))],
        cost_estimate=cost(0, 3 * width * units),
        compiler_params=pltpu.CompilerParams(vmem_limit_bytes=24 * 2**20),
        name="load_weights",
    )(gate, upper)


def weave(value, capacity, upper):
    blank = jnp.zeros((capacity, value.shape[1]), value.dtype)
    parts = []
    for p in range(value.shape[0] // capacity):
        part = value[p * capacity : (p + 1) * capacity]
        parts += [part, blank] if upper else [blank, part]
    return jnp.concatenate(parts, axis=0)


def hidden_kernel(capacity, offsets, swapped_ref, *refs):
    pieces = len(offsets)
    piece_refs = refs[:pieces]
    gate_ref, head_ref, upper_hbm, lower_hbm = refs[pieces : pieces + 4]
    keep_ref, send_ref, score_ref, delta_ref, hidden_ref, tail_ref, lower_ref, sems = refs[pieces + 4 :]
    width, units = gate_ref.shape
    middle_row = head_ref.shape[0]
    tail_copy = pltpu.make_async_copy(upper_hbm.at[middle_row:], tail_ref, sems.at[0])
    lower_copy = pltpu.make_async_copy(lower_hbm, lower_ref, sems.at[1])
    tail_copy.start()
    lower_copy.start()
    half = keep_ref.shape[0]
    across = (((1,), (1,)), ((), ()))

    def rows(start, stop):
        return jnp.concatenate([ref[:, start:stop] for ref in piece_refs], axis=0)

    def upper_rows(value):
        return jnp.concatenate(
            [value[2 * p * capacity : (2 * p + 1) * capacity] for p in range(pieces)], axis=0
        )

    def lower_rows(value):
        return jnp.concatenate(
            [value[(2 * p + 1) * capacity : (2 * p + 2) * capacity] for p in range(pieces)], axis=0
        )

    def order(value, wanted):
        lists = [
            jnp.concatenate(
                [value[offsets.index(o) * capacity : (offsets.index(o) + 1) * capacity] for o in chosen], axis=0
            )
            for chosen in wanted
        ]
        return jnp.where(swapped_ref[0] == 1, lists[1], lists[0])

    chips = [4 * x for x in range(pieces // 4)]
    kept = ([x | c for x in chips for c in (0, 2)], [x | c | 1 for x in chips for c in (2, 0)])
    sent = ([x | c | 1 for x in chips for c in (0, 2)], [x | c for x in chips for c in (2, 0)])
    gate_pre = upper_rows(jnp.dot(rows(0, width), gate_ref[...], preferred_element_type=jnp.float32))
    up_value = jnp.dot(rows(0, middle_row), head_ref[...], preferred_element_type=jnp.float32)
    tail_copy.wait()
    up_value = upper_rows(
        up_value + jnp.dot(rows(middle_row, width), tail_ref[...], preferred_element_type=jnp.float32)
    )
    lower_copy.wait()
    grad_hidden = lower_rows(lax.dot_general(rows(0, width), lower_ref[...], across, preferred_element_type=jnp.float32))
    sigma_gate = jax.nn.sigmoid(gate_pre)
    swish = gate_pre * sigma_gate
    hidden = swish * up_value
    scores = jnp.sum(hidden * grad_hidden, axis=1, keepdims=True)
    delta_gate = grad_hidden * up_value * sigma_gate * (1.0 + gate_pre * (1.0 - sigma_gate))
    delta_up = grad_hidden * swish

    marks = jnp.concatenate([ref[:, width:].astype(jnp.float32)[:capacity] for ref in piece_refs], axis=0)
    gate_rows = jnp.concatenate([order(delta_gate, kept), order(delta_gate, sent)]).astype(jnp.bfloat16)
    upper_part = jnp.concatenate([order(delta_up, kept), order(delta_up, sent)]).astype(jnp.bfloat16)
    for part, ref in ((slice(0, middle_row), head_ref), (slice(middle_row, width), tail_ref)):
        partial_rows = lax.dot_general(
            gate_rows, gate_ref[part], across, preferred_element_type=jnp.float32
        ) + lax.dot_general(upper_part, ref[...], across, preferred_element_type=jnp.float32)
        keep_ref[:, part] = partial_rows[:half]
        send_ref[:, part] = partial_rows[half:].astype(jnp.bfloat16)
    keep_ref[:, width:] = order(marks, kept)
    score_ref[...] = jnp.broadcast_to(scores[:half], (half, LANES))
    rest = scores[half:]
    high = rest.astype(jnp.bfloat16).astype(jnp.float32)
    middle = (rest - high).astype(jnp.bfloat16).astype(jnp.float32)
    low = rest - high - middle
    lane = lax.broadcasted_iota(jnp.int32, (half, LANES), 1)
    parts = jnp.where(lane == 0, high, jnp.where(lane == 1, middle, jnp.where(lane == 2, low, 0.0)))
    send_ref[:, width:] = parts.astype(jnp.bfloat16)
    delta_ref[:, :units] = weave(delta_gate, capacity, True).astype(jnp.bfloat16)
    delta_ref[:, units:] = weave(delta_up, capacity, True).astype(jnp.bfloat16)
    hidden_ref[...] = weave(hidden, capacity, False).astype(jnp.bfloat16)


def hidden_pass(swapped, pieces, offsets, gate, head, upper, lower, capacity):
    width, units = gate.shape
    count = len(pieces)
    half = count * capacity // 2
    rows = 2 * count * capacity
    return pl.pallas_call(
        functools.partial(hidden_kernel, capacity, offsets),
        out_shape=[
            shape_of((half, width + LANES), jnp.float32),
            shape_of((half, width + LANES), jnp.bfloat16),
            shape_of((half, LANES), jnp.float32),
            shape_of((rows, 2 * units), jnp.bfloat16),
            shape_of((rows, units), jnp.bfloat16),
        ],
        in_specs=[pl.BlockSpec(memory_space=pltpu.SMEM)] + [VMEM] * (count + 2) + [HBM] * 2,
        out_specs=[VMEM] * 5,
        scratch_shapes=[
            pltpu.VMEM((width - head.shape[0], units), jnp.bfloat16),
            pltpu.VMEM((units, width), jnp.bfloat16),
            pltpu.SemaphoreType.DMA((2,)),
        ],
        cost_estimate=cost(10 * rows * width * units, 6 * width * units),
        compiler_params=pltpu.CompilerParams(vmem_limit_bytes=24 * 2**20),
        name="hidden_pass",
    )(swapped, *pieces, gate, head, upper, lower)


def join_kernel(width, messages, keep_ref, score_ref, recv_ref, *out_refs):
    for j in range(messages):
        rows = out_refs[j].shape[0]
        part = slice(j * rows, (j + 1) * rows)
        other = recv_ref[part, :width].astype(jnp.float32)
        out_refs[j][:, :width] = (keep_ref[part, :width] + other).astype(jnp.bfloat16)
        out_refs[j][:, width:] = keep_ref[part, width:].astype(jnp.bfloat16)
    extra = recv_ref[:, width:].astype(jnp.float32)
    out_refs[messages][...] = score_ref[...] + jnp.sum(extra, axis=1, keepdims=True)


def join_cores(keep, scores, recv, messages):
    half, wide = keep.shape
    return pl.pallas_call(
        functools.partial(join_kernel, wide - LANES, messages),
        out_shape=[shape_of((half // messages, wide), jnp.bfloat16)] * messages
        + [shape_of((half, LANES), jnp.float32)],
        in_specs=[VMEM] * 3,
        out_specs=[VMEM] * (messages + 1),
        cost_estimate=cost(2 * half * wide, 8 * half * wide),
        compiler_params=pltpu.CompilerParams(vmem_limit_bytes=8 * 2**20),
        name="join_cores",
    )(keep, scores, recv)


def weights_kernel(pieces, step, *refs):
    piece_refs = refs[:pieces]
    delta_ref, hidden_ref, gate_out, upper_out, lower_out = refs[pieces:]
    start = pl.multiple_of(pl.program_id(0) * step, step)
    rows = jnp.concatenate([ref[:, pl.ds(start, step)] for ref in piece_refs], axis=0)
    down = (((0,), (0,)), ((), ()))
    both = lax.dot_general(rows, delta_ref[...], down, preferred_element_type=jnp.float32)
    units = gate_out.shape[1]
    gate_out[...] = both[:, :units].astype(jnp.bfloat16)
    upper_out[...] = both[:, units:].astype(jnp.bfloat16)
    lower_out[...] = lax.dot_general(
        hidden_ref[...], rows, down, preferred_element_type=jnp.float32
    ).astype(jnp.bfloat16)


def weight_grads(pieces, delta, hidden, step):
    width = pieces[0].shape[1] - LANES
    rows, units = hidden.shape
    count = len(pieces)

    def whole(array):
        return pl.BlockSpec(array.shape, lambda i: (0, 0))

    return pl.pallas_call(
        functools.partial(weights_kernel, count, step),
        grid=(width // step,),
        out_shape=[
            shape_of((width, units), jnp.bfloat16),
            shape_of((width, units), jnp.bfloat16),
            shape_of((units, width), jnp.bfloat16),
        ],
        in_specs=[whole(array) for array in (*pieces, delta, hidden)],
        out_specs=[
            pl.BlockSpec((step, units), lambda i: (i, 0)),
            pl.BlockSpec((step, units), lambda i: (i, 0)),
            pl.BlockSpec((units, step), lambda i: (0, i)),
        ],
        cost_estimate=cost(6 * rows * width * units, 6 * width * units),
        compiler_params=pltpu.CompilerParams(vmem_limit_bytes=24 * 2**20),
        name="weight_grads",
    )(*pieces, delta, hidden)


def score_kernel(capacity, own_ref, ids_ref, weight_ref, select_ref, *refs):
    out_ref = refs[-1]
    chosen, _, tokens = ids_ref.shape
    sums = []
    for j in range(2):
        part = slice(j * capacity, (j + 1) * capacity)
        picked = select_ref[part].astype(jnp.float32) * refs[j][:, :1]
        sums.append(jnp.sum(picked, axis=0, keepdims=True))
    for k in range(chosen):
        value = jnp.zeros((1, tokens), jnp.float32)
        for j in range(2):
            value = jnp.where(ids_ref[k] == (own_ref[0] ^ j), sums[j], value)
        out_ref[k] = value / weight_ref[k]


def score_grads(own, ids, weights, select, scores, capacity):
    return pl.pallas_call(
        functools.partial(score_kernel, capacity),
        out_shape=shape_of(weights.shape, jnp.float32),
        in_specs=[pl.BlockSpec(memory_space=pltpu.SMEM)] + [VMEM] * 5,
        out_specs=VMEM,
        cost_estimate=cost(1000, 1000),
        compiler_params=pltpu.CompilerParams(vmem_limit_bytes=4 * 2**20),
        name="score_grads",
    )(own, ids, weights, select, *scores)


def total_kernel(messages, *refs):
    own_ref, other_ref = refs[messages:]
    capacity, wide = own_ref.shape
    width = wide - LANES
    total = refs[0][:, :width].astype(jnp.float32)
    for ref in refs[1:messages]:
        total = total + ref[:, :width].astype(jnp.float32)
    marks = refs[0][:, width:].astype(jnp.float32)
    own_ref[:, :width] = total[:capacity].astype(jnp.bfloat16)
    own_ref[:, width:] = marks[:capacity].astype(jnp.bfloat16)
    other_ref[:, :width] = total[capacity:].astype(jnp.bfloat16)
    other_ref[:, width:] = marks[capacity:].astype(jnp.bfloat16)


def total_rows(arrays):
    rows, wide = arrays[0].shape
    return pl.pallas_call(
        functools.partial(total_kernel, len(arrays)),
        out_shape=[shape_of((rows // 2, wide), jnp.bfloat16)] * 2,
        in_specs=[VMEM] * len(arrays),
        out_specs=[VMEM] * 2,
        cost_estimate=cost(rows * wide, 4 * rows * wide),
        compiler_params=pltpu.CompilerParams(vmem_limit_bytes=4 * 2**20),
        name="total_rows",
    )(*arrays)


def spread_kernel(step, own_ref, other_ref, out_ref):
    tokens = out_ref.shape[0]
    capacity, wide = own_ref.shape
    width = wide - LANES
    start = pl.multiple_of(pl.program_id(0) * step, step)
    marks = jnp.concatenate([ref[:, width:].astype(jnp.float32) for ref in (own_ref, other_ref)], axis=0)
    lane = lax.broadcasted_iota(jnp.int32, marks.shape, 1)
    number = jnp.sum(jnp.where(lane == 0, marks * 256.0, jnp.where(lane == 1, marks, 0.0)), axis=1, keepdims=True)
    token = lax.broadcasted_iota(jnp.int32, (2 * capacity, tokens), 1).astype(jnp.float32)
    select = jnp.where(token + 1.0 == number, 1.0, 0.0).astype(jnp.bfloat16)
    rows = jnp.concatenate(
        [ref[:, pl.ds(start, step)].astype(jnp.float32) for ref in (own_ref, other_ref)], axis=0
    ).astype(jnp.bfloat16)
    out_ref[...] = lax.dot_general(
        select, rows, (((0,), (0,)), ((), ())), preferred_element_type=jnp.float32
    ).astype(jnp.bfloat16)


def spread_rows(own_rows, other_rows, tokens, step):
    capacity, wide = own_rows.shape
    width = wide - LANES
    whole = pl.BlockSpec(own_rows.shape, lambda i: (0, 0))
    return pl.pallas_call(
        functools.partial(spread_kernel, step),
        grid=(width // step,),
        out_shape=shape_of((tokens, width), jnp.bfloat16),
        in_specs=[whole, whole],
        out_specs=pl.BlockSpec((tokens, step), lambda i: (0, i)),
        cost_estimate=cost(4 * capacity * tokens * width, 2 * tokens * width),
        compiler_params=pltpu.CompilerParams(vmem_limit_bytes=16 * 2**20),
        name="spread_rows",
    )(own_rows, other_rows)


def pairwise_shards(block_input, output_grad, expert_ids, gate_weights, gate_proj, up_proj, down_proj):
    tokens = block_input.shape[1]
    width = block_input.shape[2]
    capacity = tokens // 16
    count = 2 * lax.axis_size("dp")
    plane = [offset for offset in range(count) if not offset & 2]
    offsets = plane + [offset | 2 for offset in plane]
    expert_index = lax.axis_index("expert").astype(jnp.int32)
    core_index = lax.axis_index("dp").astype(jnp.int32) & 1
    own = expert_index.reshape(1)
    swapped = (expert_index ^ core_index).reshape(1)
    ids = jnp.transpose(expert_ids, (2, 0, 1))
    weights = jnp.transpose(gate_weights, (2, 0, 1))
    stay = functools.partial(pltpu.with_memory_space_constraint, memory_space=pltpu.HBM)
    *sends, select = pick_rows(
        own, stay(ids), stay(weights), stay(block_input[0]), stay(output_grad[0]), capacity
    )
    upper, lower = stay(up_proj[0, 0]), stay(down_proj[0, 0])
    gate, head = load_weights(stay(gate_proj[0, 0]), upper)
    mine = {0: sends[0]}
    for offset in sorted(plane[1:], reverse=True):
        mine[offset] = swap(sends[offset % 2], offset)
    theirs = {offset: swap(mine[offset], 2) for offset in plane}
    pieces = [mine[offset] for offset in plane] + [theirs[offset] for offset in plane]
    keep, send, scores, delta, hidden = hidden_pass(
        swapped, pieces, offsets, gate, head, upper, lower, capacity
    )
    recv = swap(send, 2)
    chips = count // 4
    *joined, scores = join_cores(keep, scores, recv, chips)
    messages = [send_back(joined[x], x) for x in range(chips)]
    gate_grad, upper_grad, lower_grad = weight_grads(pieces, delta, hidden, width // 2)
    score_rows = {offset: scores[i * capacity : (i + 1) * capacity, :1] for i, offset in enumerate(plane)}
    bit = count // 2
    while bit > 2:
        low = [offset for offset in score_rows if not offset & bit]
        moved = swap(jnp.concatenate([score_rows[offset | bit] for offset in low]), bit)
        score_rows = {
            offset: score_rows[offset] + moved[i * capacity : (i + 1) * capacity]
            for i, offset in enumerate(low)
        }
        bit //= 2
    score_list = [score_rows[0], swap(score_rows[1], 1)]
    weight_grad = score_grads(own, ids, weights, select, score_list, capacity)
    own_rows, other_rows = total_rows(messages)
    received = spread_rows(own_rows, swap(other_rows, 2), tokens, width // 2)
    return (
        received[None],
        jnp.transpose(weight_grad, (1, 2, 0)),
        gate_grad[None, None],
        upper_grad[None, None],
        lower_grad[None, None],
    )


def shifted(value, axis, steps):
    count = lax.axis_size(axis)
    pairs = [(source, (source + steps) % count) for source in range(count)]
    return lax.ppermute(value, axis, pairs)


def slot_tables(chosen_ids, experts, capacity):
    tok_count, chosen = chosen_ids.shape
    flat_ids = chosen_ids.reshape(-1)
    columns = jnp.arange(experts, dtype=jnp.int32)
    onehot = (flat_ids[:, None] == columns[None, :]).astype(jnp.int32)
    earlier = jnp.cumsum(onehot, axis=0) - onehot
    slot_rank = jnp.sum(earlier * onehot, axis=1)
    kept_pair = (flat_ids < experts) & (slot_rank < capacity)
    slot_index = jnp.where(kept_pair, flat_ids * capacity + slot_rank, experts * capacity)
    slot_rows = jnp.arange(experts * capacity, dtype=jnp.int32)
    placed = slot_index[None, :] == slot_rows[:, None]
    pair_index = jnp.arange(tok_count * chosen, dtype=jnp.int32)
    source_pair = jnp.sum(jnp.where(placed, pair_index[None, :], 0), axis=1)
    filled = jnp.any(placed, axis=1)
    return (slot_index, source_pair, filled)


def general_shards(block_input, output_grad, expert_ids, gate_weights, gate_proj, up_proj, down_proj):
    acts_local = block_input[0]
    grad_local = output_grad[0]
    chosen_ids = expert_ids[0]
    route_weight = gate_weights[0]
    tok_count, chosen = chosen_ids.shape
    width = acts_local.shape[1]
    local_count = gate_proj.shape[1]
    dp_count = lax.axis_size("dp")
    expert_count = lax.axis_size("expert")
    experts = local_count * expert_count
    capacity = tok_count // 16
    slot_index, source_pair, filled = slot_tables(chosen_ids, experts, capacity)
    source_token = source_pair // chosen
    slot_weight = route_weight.reshape(-1)[source_pair]
    send_acts = jnp.where(filled[:, None], acts_local[source_token], jnp.zeros((), jnp.bfloat16))
    scaled = slot_weight[:, None] * grad_local[source_token].astype(jnp.float32)
    send_grad = jnp.where(filled[:, None], scaled, 0.0).astype(jnp.bfloat16)
    send_acts = send_acts.reshape(experts, capacity, width)
    send_grad = send_grad.reshape(experts, capacity, width)
    acts_copies = jnp.broadcast_to(send_acts[None], (dp_count,) + send_acts.shape).reshape(
        dp_count * experts, capacity, width
    )
    grad_copies = jnp.broadcast_to(send_grad[None], (dp_count,) + send_grad.shape).reshape(
        dp_count * experts, capacity, width
    )
    recv_acts, recv_grad = (
        lax.all_to_all(acts_copies, ("dp", "expert"), split_axis=0, concat_axis=1, tiled=True),
        lax.all_to_all(grad_copies, ("dp", "expert"), split_axis=0, concat_axis=1, tiled=True),
    )
    gate_local = gate_proj[0]
    upper_local = up_proj[0]
    lower_local = down_proj[0]
    gate_pre = jnp.einsum("erd,edh->erh", recv_acts, gate_local, preferred_element_type=jnp.float32)
    up_value = jnp.einsum(
        "erd,edh->erh", recv_acts, upper_local, preferred_element_type=jnp.float32
    )
    grad_hidden = jnp.einsum(
        "erd,ehd->erh", recv_grad, lower_local, preferred_element_type=jnp.float32
    )
    sigma_gate = jax.nn.sigmoid(gate_pre)
    swish = gate_pre * sigma_gate
    hidden = swish * up_value
    scores = jnp.sum(hidden * grad_hidden, axis=2)
    lower_grad = jnp.einsum(
        "erh,erd->ehd", hidden.astype(jnp.bfloat16), recv_grad, preferred_element_type=jnp.float32
    ).astype(jnp.bfloat16)
    delta_gate = (
        grad_hidden * up_value * sigma_gate * (1.0 + gate_pre * (1.0 - sigma_gate))
    ).astype(jnp.bfloat16)
    delta_up = (grad_hidden * swish).astype(jnp.bfloat16)
    gate_grad = jnp.einsum(
        "erd,erh->edh", recv_acts, delta_gate, preferred_element_type=jnp.float32
    ).astype(jnp.bfloat16)
    upper_grad = jnp.einsum(
        "erd,erh->edh", recv_acts, delta_up, preferred_element_type=jnp.float32
    ).astype(jnp.bfloat16)
    partial_value = jnp.einsum(
        "erh,edh->erd", delta_gate, gate_local, preferred_element_type=jnp.float32
    ) + jnp.einsum("erh,edh->erd", delta_up, upper_local, preferred_element_type=jnp.float32)
    back_rows, back_scores = (
        lax.all_to_all(partial_value, ("dp", "expert"), split_axis=1, concat_axis=0, tiled=True),
        lax.all_to_all(scores, ("dp", "expert"), split_axis=1, concat_axis=0, tiled=True),
    )
    slot_grad = jnp.sum(back_rows.reshape(dp_count, experts * capacity, width), axis=0).astype(
        jnp.bfloat16
    )
    slot_scores = jnp.sum(back_scores.reshape(dp_count, experts * capacity), axis=0)
    token_rows = jnp.arange(tok_count, dtype=jnp.int32)
    token_map = ((source_token[:, None] == token_rows[None, :]) & filled[:, None]).astype(
        jnp.bfloat16
    )
    input_grad = jnp.einsum(
        "st,sd->td", token_map, slot_grad, preferred_element_type=jnp.float32
    ).astype(jnp.bfloat16)
    padded_scores = jnp.concatenate([slot_scores, jnp.zeros((1,), jnp.float32)])
    weight_grad = (padded_scores[slot_index] / route_weight.reshape(-1)).reshape(tok_count, chosen)
    received = shifted(input_grad, "pipe", -1)
    return (received[None], weight_grad[None], gate_grad[None], upper_grad[None], lower_grad[None])


def solution(mesh):
    in_specs = (
        P("pipe", ("dp", "expert"), None),
        P("pipe", ("dp", "expert"), None),
        P("pipe", ("dp", "expert"), None),
        P("pipe", ("dp", "expert"), None),
        P("pipe", "expert", None, "dp"),
        P("pipe", "expert", None, "dp"),
        P("pipe", "expert", "dp", None),
    )
    out_specs = (
        P("pipe", ("dp", "expert"), None),
        P("pipe", ("dp", "expert"), None),
        P("pipe", "expert", None, "dp"),
        P("pipe", "expert", None, "dp"),
        P("pipe", "expert", "dp", None),
    )
    dp_count, expert_count = mesh.shape["dp"], mesh.shape["expert"]

    def shards(*arrays):
        pairwise = (
            expert_count == 2
            and dp_count * expert_count <= PAIRWISE_MAX
            and dp_count > 1
            and power_of_two(dp_count)
            and arrays[4].shape[1] == 1
        )
        return (pairwise_shards if pairwise else general_shards)(*arrays)

    return jax.shard_map(shards, mesh=mesh, in_specs=in_specs, out_specs=out_specs, check_vma=False)
```

```python
import functools

import jax
import jax.numpy as jnp
from jax import lax
from jax.experimental import pallas as pl
from jax.experimental.pallas import tpu as pltpu
from jax.sharding import PartitionSpec as P


PAIRWISE_MAX = 8
LANES = 128
VMEM = pl.BlockSpec(memory_space=pltpu.VMEM)
HBM = pl.BlockSpec(memory_space=pltpu.HBM)


def shape_of(shape, dtype):
    return jax.ShapeDtypeStruct(shape, dtype)


def cost(flops, bytes_moved):
    return pl.CostEstimate(flops=flops, bytes_accessed=bytes_moved, transcendentals=0)


def power_of_two(number):
    return number > 0 and number & (number - 1) == 0


def swap(value, offset):
    count = lax.axis_size("dp") * lax.axis_size("expert")
    return lax.ppermute(value, ("dp", "expert"), [(i, i ^ offset) for i in range(count)])


def send_back(value, across):
    sections = lax.axis_size("pipe")
    chips = lax.axis_size("dp") // 2
    pairs = []
    for s in range(sections):
        for x in range(chips):
            for core in range(2):
                for expert in range(2):
                    source = (s * chips + x) * 4 + 2 * core + expert
                    target = (((s - 1) % sections) * chips + (x ^ across)) * 4 + 2 * expert + core
                    pairs.append((source, target))
    return lax.ppermute(value, ("pipe", "dp", "expert"), pairs)


def pick_kernel(capacity, own_ref, ids_hbm, weight_hbm, acts_hbm, grad_hbm, *refs):
    outs = refs[:2]
    select_ref, ids_ref, weight_ref, acts_ref, grad_ref, sems = refs[2:]
    copies = [
        pltpu.make_async_copy(source, target, sems.at[i])
        for i, (source, target) in enumerate(
            [(ids_hbm, ids_ref), (weight_hbm, weight_ref), (acts_hbm, acts_ref), (grad_hbm, grad_ref)]
        )
    ]
    for copy in copies:
        copy.start()
    chosen, _, tokens = ids_ref.shape
    width = acts_ref.shape[1]
    rows = 2 * capacity
    row = lax.broadcasted_iota(jnp.int32, (rows, tokens), 0)
    row_expert = (row // capacity) ^ own_ref[0]
    before = lax.broadcasted_iota(jnp.int32, (tokens, tokens), 0)
    after = lax.broadcasted_iota(jnp.int32, (tokens, tokens), 1)
    earlier = jnp.where(before < after, 1.0, 0.0).astype(jnp.bfloat16)
    slot = (row % capacity).astype(jnp.float32)
    token = lax.broadcasted_iota(jnp.int32, (rows, tokens), 1).astype(jnp.float32)
    lane = lax.broadcasted_iota(jnp.int32, (rows, LANES), 1)
    taken = jnp.zeros((rows, tokens), jnp.float32)
    scale = jnp.zeros((rows, tokens), jnp.float32)
    copies[0].wait()
    copies[1].wait()
    for k in range(chosen):
        same = ids_ref[k] == row_expert
        taken = jnp.where(same, 1.0, taken)
        scale = jnp.where(same, weight_ref[k], scale)
    rank = jnp.dot(taken.astype(jnp.bfloat16), earlier, preferred_element_type=jnp.float32)
    select = jnp.where(rank == slot, taken, 0.0)
    row_scale = jnp.sum(select * scale, axis=1, keepdims=True)
    number = jnp.sum(select * (token + 1.0), axis=1, keepdims=True)
    high = jnp.floor(number / 256.0)
    marks = jnp.where(lane == 0, high, jnp.where(lane == 1, number - 256.0 * high, 0.0))
    select = select.astype(jnp.bfloat16)
    select_ref[...] = select
    copies[2].wait()
    acts_rows = jnp.dot(select, acts_ref[...], preferred_element_type=jnp.float32)
    copies[3].wait()
    grad_rows = jnp.dot(select, grad_ref[...], preferred_element_type=jnp.float32) * row_scale
    for j in range(2):
        part = slice(j * capacity, (j + 1) * capacity)
        outs[j][:, :width] = jnp.concatenate([acts_rows[part], grad_rows[part]], axis=0).astype(jnp.bfloat16)
        outs[j][:, width:] = jnp.concatenate([marks[part]] * 2, axis=0).astype(jnp.bfloat16)


def pick_rows(own, ids, weights, acts, grads, capacity):
    tokens, width = acts.shape
    group = shape_of((2 * capacity, width + LANES), jnp.bfloat16)
    return pl.pallas_call(
        functools.partial(pick_kernel, capacity),
        out_shape=[group, group, shape_of((2 * capacity, tokens), jnp.bfloat16)],
        in_specs=[pl.BlockSpec(memory_space=pltpu.SMEM)] + [HBM] * 4,
        out_specs=[VMEM] * 3,
        scratch_shapes=[
            pltpu.VMEM(ids.shape, jnp.int32),
            pltpu.VMEM(weights.shape, jnp.float32),
            pltpu.VMEM((tokens, width), jnp.bfloat16),
            pltpu.VMEM((tokens, width), jnp.bfloat16),
            pltpu.SemaphoreType.DMA((4,)),
        ],
        cost_estimate=cost(8 * capacity * tokens * width, 4 * tokens * width),
        compiler_params=pltpu.CompilerParams(vmem_limit_bytes=16 * 2**20),
        name="pick_rows",
    )(own, ids, weights, acts, grads)


def load_kernel(gate_hbm, upper_hbm, gate_ref, upper_ref, sems):
    gate_copy = pltpu.make_async_copy(gate_hbm, gate_ref, sems.at[0])
    upper_copy = pltpu.make_async_copy(upper_hbm.at[: upper_ref.shape[0]], upper_ref, sems.at[1])
    gate_copy.start()
    upper_copy.start()
    gate_copy.wait()
    upper_copy.wait()


def load_weights(gate, upper):
    width, units = gate.shape
    return pl.pallas_call(
        load_kernel,
        out_shape=[shape_of((width, units), gate.dtype), shape_of((width // 2, units), upper.dtype)],
        in_specs=[HBM] * 2,
        out_specs=[VMEM] * 2,
        scratch_shapes=[pltpu.SemaphoreType.DMA((2,))],
        cost_estimate=cost(0, 3 * width * units),
        compiler_params=pltpu.CompilerParams(vmem_limit_bytes=24 * 2**20),
        name="load_weights",
    )(gate, upper)


def weave(value, capacity, upper):
    blank = jnp.zeros((capacity, value.shape[1]), value.dtype)
    parts = []
    for p in range(value.shape[0] // capacity):
        part = value[p * capacity : (p + 1) * capacity]
        parts += [part, blank] if upper else [blank, part]
    return jnp.concatenate(parts, axis=0)


def chain(steps):
    count = [0, 0]
    staged = []
    for unit, weights, turned, left, total in steps:
        staged.append((unit, count[unit] % 2))
        count[unit] += 1
    ahead = 2
    for i in range(len(steps) + ahead):
        if i < len(steps):
            unit, weights, turned, _, _ = steps[i]
            pltpu.matmul_push_rhs(weights(), staging_register=staged[i][1], mxu_index=unit, transpose=turned)
        if i >= ahead:
            _, _, _, left, total = steps[i - ahead]
            pltpu.matmul_acc_lhs(total, left(), load_staged_rhs=staged[i - ahead][1])


def hidden_kernel(capacity, offsets, swapped_ref, *refs):
    pieces = len(offsets)
    piece_refs = refs[:pieces]
    gate_ref, head_ref, upper_hbm, lower_hbm = refs[pieces : pieces + 4]
    keep_ref, send_ref, score_ref, delta_ref, hidden_ref = refs[pieces + 4 : pieces + 9]
    tail_ref, lower_ref, sems = refs[pieces + 9 :]
    width, units = gate_ref.shape
    middle_row = head_ref.shape[0]
    rows = pieces * capacity
    half = rows // 2
    tile = units
    tail_copy = pltpu.make_async_copy(upper_hbm.at[middle_row:], tail_ref, sems.at[0])
    lower_copies = [
        pltpu.make_async_copy(lower_hbm.at[:, part], lower_ref.at[:, part], sems.at[1 + i])
        for i, part in enumerate((slice(0, middle_row), slice(middle_row, width)))
    ]
    tail_copy.start()
    for copy in lower_copies:
        copy.start()

    def acts(start):
        return jnp.concatenate([ref[:capacity, start : start + tile] for ref in piece_refs], axis=0)

    def grads(start):
        return jnp.concatenate([ref[capacity:, start : start + tile] for ref in piece_refs], axis=0)

    def order(value, wanted):
        lists = [
            jnp.concatenate(
                [value[offsets.index(o) * capacity : (offsets.index(o) + 1) * capacity] for o in chosen], axis=0
            )
            for chosen in wanted
        ]
        return jnp.where(swapped_ref[0] == 1, lists[1], lists[0])

    chips = [4 * x for x in range(pieces // 4)]
    kept = ([x | c for x in chips for c in (0, 2)], [x | c | 1 for x in chips for c in (2, 0)])
    sent = ([x | c | 1 for x in chips for c in (0, 2)], [x | c for x in chips for c in (2, 0)])

    def at(ref, start):
        return lambda: ref[start : start + tile]

    def at_column(ref, start):
        return lambda: ref[:, start : start + tile]

    def forward(first, second):
        def steps(starts, upper_ref, base):
            result = []
            for start in starts:
                left = functools.partial(acts, start)
                result.append((0, at(gate_ref, start), False, left, first))
                result.append((1, at(upper_ref, start - base), False, left, second))
            return result

        chain(steps(range(0, middle_row, tile), head_ref, 0))
        tail_copy.wait()
        chain(steps(range(middle_row, width, tile), tail_ref, middle_row))
        return pltpu.matmul_pop(first), pltpu.matmul_pop(second)

    def backward(first, second):
        totals = (first, second)

        def steps(starts):
            return [
                (i % 2, at_column(lower_ref, start), True, functools.partial(grads, start), totals[i % 2])
                for i, start in enumerate(starts)
            ]

        lower_copies[0].wait()
        chain(steps(range(0, middle_row, tile)))
        lower_copies[1].wait()
        chain(steps(range(middle_row, width, tile)))
        return pltpu.matmul_pop(first) + pltpu.matmul_pop(second)

    totals = [pltpu.ACC(unit)((rows, tile), jnp.float32) for unit in range(2)]
    gate_pre, up_value = pl.run_scoped(forward, *totals)
    grad_hidden = pl.run_scoped(backward, *totals)
    sigma_gate = jax.nn.sigmoid(gate_pre)
    swish = gate_pre * sigma_gate
    hidden = swish * up_value
    scores = jnp.sum(hidden * grad_hidden, axis=1, keepdims=True)
    delta_gate = grad_hidden * up_value * sigma_gate * (1.0 + gate_pre * (1.0 - sigma_gate))
    delta_up = grad_hidden * swish
    marks = jnp.concatenate([ref[:, width:].astype(jnp.float32)[:capacity] for ref in piece_refs], axis=0)
    gate_part = jnp.concatenate([order(delta_gate, kept), order(delta_gate, sent)]).astype(jnp.bfloat16)
    upper_part = jnp.concatenate([order(delta_up, kept), order(delta_up, sent)]).astype(jnp.bfloat16)
    keep_ref[:, width:] = order(marks, kept)

    def back(*accs):
        starts = list(range(0, width, tile))
        for group in range(0, len(starts), 4):
            steps = []
            for source in range(2):
                for i, start in enumerate(starts[group : group + 4]):
                    unit = i % 2
                    if source == 0:
                        weights, left = at(gate_ref, start), gate_part
                    elif start < middle_row:
                        weights, left = at(head_ref, start), upper_part
                    else:
                        weights, left = at(tail_ref, start - middle_row), upper_part
                    total = accs[2 * ((group // 4 * 2 + i // 2) % 2) + unit]
                    steps.append((unit, weights, True, lambda left=left: left, total))
            ordered = [steps[i] for i in (0, 1, 4, 5, 2, 3, 6, 7) if i < len(steps)] if len(steps) == 8 else steps
            chain(ordered)
            for i, start in enumerate(starts[group : group + 4]):
                total = accs[2 * ((group // 4 * 2 + i // 2) % 2) + i % 2]
                block = pltpu.matmul_pop(total)
                keep_ref[:, start : start + tile] = block[:half]
                send_ref[:, start : start + tile] = block[half:].astype(jnp.bfloat16)

    pl.run_scoped(back, *totals, *totals)
    score_ref[...] = jnp.broadcast_to(scores[:half], (half, LANES))
    rest = scores[half:]
    high = rest.astype(jnp.bfloat16).astype(jnp.float32)
    middle = (rest - high).astype(jnp.bfloat16).astype(jnp.float32)
    low = rest - high - middle
    lane = lax.broadcasted_iota(jnp.int32, (half, LANES), 1)
    parts = jnp.where(lane == 0, high, jnp.where(lane == 1, middle, jnp.where(lane == 2, low, 0.0)))
    send_ref[:, width:] = parts.astype(jnp.bfloat16)
    delta_ref[:, :units] = weave(delta_gate, capacity, True).astype(jnp.bfloat16)
    delta_ref[:, units:] = weave(delta_up, capacity, True).astype(jnp.bfloat16)
    hidden_ref[...] = weave(hidden, capacity, False).astype(jnp.bfloat16)


def hidden_pass(swapped, pieces, offsets, gate, head, upper, lower, capacity):
    width, units = gate.shape
    count = len(pieces)
    half = count * capacity // 2
    rows = 2 * count * capacity
    return pl.pallas_call(
        functools.partial(hidden_kernel, capacity, offsets),
        out_shape=[
            shape_of((half, width + LANES), jnp.float32),
            shape_of((half, width + LANES), jnp.bfloat16),
            shape_of((half, LANES), jnp.float32),
            shape_of((rows, 2 * units), jnp.bfloat16),
            shape_of((rows, units), jnp.bfloat16),
        ],
        in_specs=[pl.BlockSpec(memory_space=pltpu.SMEM)] + [VMEM] * (count + 2) + [HBM] * 2,
        out_specs=[VMEM] * 5,
        scratch_shapes=[
            pltpu.VMEM((width - head.shape[0], units), jnp.bfloat16),
            pltpu.VMEM((units, width), jnp.bfloat16),
            pltpu.SemaphoreType.DMA((3,)),
        ],
        cost_estimate=cost(10 * rows * width * units, 6 * width * units),
        compiler_params=pltpu.CompilerParams(vmem_limit_bytes=24 * 2**20),
        name="hidden_pass",
    )(swapped, *pieces, gate, head, upper, lower)


def join_kernel(width, messages, keep_ref, score_ref, recv_ref, *out_refs):
    for j in range(messages):
        rows = out_refs[j].shape[0]
        part = slice(j * rows, (j + 1) * rows)
        other = recv_ref[part, :width].astype(jnp.float32)
        out_refs[j][:, :width] = (keep_ref[part, :width] + other).astype(jnp.bfloat16)
        out_refs[j][:, width:] = keep_ref[part, width:].astype(jnp.bfloat16)
    extra = recv_ref[:, width:].astype(jnp.float32)
    out_refs[messages][...] = score_ref[...] + jnp.sum(extra, axis=1, keepdims=True)


def join_cores(keep, scores, recv, messages):
    half, wide = keep.shape
    return pl.pallas_call(
        functools.partial(join_kernel, wide - LANES, messages),
        out_shape=[shape_of((half // messages, wide), jnp.bfloat16)] * messages
        + [shape_of((half, LANES), jnp.float32)],
        in_specs=[VMEM] * 3,
        out_specs=[VMEM] * (messages + 1),
        cost_estimate=cost(2 * half * wide, 8 * half * wide),
        compiler_params=pltpu.CompilerParams(vmem_limit_bytes=8 * 2**20),
        name="join_cores",
    )(keep, scores, recv)


def weights_kernel(pieces, step, *refs):
    piece_refs = refs[:pieces]
    delta_ref, hidden_ref, gate_out, upper_out, lower_out = refs[pieces:]
    start = pl.multiple_of(pl.program_id(0) * step, step)
    rows = jnp.concatenate([ref[:, pl.ds(start, step)] for ref in piece_refs], axis=0)
    down = (((0,), (0,)), ((), ()))
    both = lax.dot_general(rows, delta_ref[...], down, preferred_element_type=jnp.float32)
    units = gate_out.shape[1]
    gate_out[...] = both[:, :units].astype(jnp.bfloat16)
    upper_out[...] = both[:, units:].astype(jnp.bfloat16)
    lower_out[...] = lax.dot_general(
        hidden_ref[...], rows, down, preferred_element_type=jnp.float32
    ).astype(jnp.bfloat16)


def weight_grads(pieces, delta, hidden, step):
    width = pieces[0].shape[1] - LANES
    rows, units = hidden.shape
    count = len(pieces)

    def whole(array):
        return pl.BlockSpec(array.shape, lambda i: (0, 0))

    return pl.pallas_call(
        functools.partial(weights_kernel, count, step),
        grid=(width // step,),
        out_shape=[
            shape_of((width, units), jnp.bfloat16),
            shape_of((width, units), jnp.bfloat16),
            shape_of((units, width), jnp.bfloat16),
        ],
        in_specs=[whole(array) for array in (*pieces, delta, hidden)],
        out_specs=[
            pl.BlockSpec((step, units), lambda i: (i, 0)),
            pl.BlockSpec((step, units), lambda i: (i, 0)),
            pl.BlockSpec((units, step), lambda i: (0, i)),
        ],
        cost_estimate=cost(6 * rows * width * units, 6 * width * units),
        compiler_params=pltpu.CompilerParams(vmem_limit_bytes=24 * 2**20),
        name="weight_grads",
    )(*pieces, delta, hidden)


def score_kernel(capacity, own_ref, ids_ref, weight_ref, select_ref, *refs):
    out_ref = refs[-1]
    chosen, _, tokens = ids_ref.shape
    sums = []
    for j in range(2):
        part = slice(j * capacity, (j + 1) * capacity)
        picked = select_ref[part].astype(jnp.float32) * refs[j][:, :1]
        sums.append(jnp.sum(picked, axis=0, keepdims=True))
    for k in range(chosen):
        value = jnp.zeros((1, tokens), jnp.float32)
        for j in range(2):
            value = jnp.where(ids_ref[k] == (own_ref[0] ^ j), sums[j], value)
        out_ref[k] = value / weight_ref[k]


def score_grads(own, ids, weights, select, scores, capacity):
    return pl.pallas_call(
        functools.partial(score_kernel, capacity),
        out_shape=shape_of(weights.shape, jnp.float32),
        in_specs=[pl.BlockSpec(memory_space=pltpu.SMEM)] + [VMEM] * 5,
        out_specs=VMEM,
        cost_estimate=cost(1000, 1000),
        compiler_params=pltpu.CompilerParams(vmem_limit_bytes=4 * 2**20),
        name="score_grads",
    )(own, ids, weights, select, *scores)


def total_kernel(messages, *refs):
    own_ref, other_ref = refs[messages:]
    capacity, wide = own_ref.shape
    width = wide - LANES
    total = refs[0][:, :width].astype(jnp.float32)
    for ref in refs[1:messages]:
        total = total + ref[:, :width].astype(jnp.float32)
    marks = refs[0][:, width:].astype(jnp.float32)
    own_ref[:, :width] = total[:capacity].astype(jnp.bfloat16)
    own_ref[:, width:] = marks[:capacity].astype(jnp.bfloat16)
    other_ref[:, :width] = total[capacity:].astype(jnp.bfloat16)
    other_ref[:, width:] = marks[capacity:].astype(jnp.bfloat16)


def total_rows(arrays):
    rows, wide = arrays[0].shape
    return pl.pallas_call(
        functools.partial(total_kernel, len(arrays)),
        out_shape=[shape_of((rows // 2, wide), jnp.bfloat16)] * 2,
        in_specs=[VMEM] * len(arrays),
        out_specs=[VMEM] * 2,
        cost_estimate=cost(rows * wide, 4 * rows * wide),
        compiler_params=pltpu.CompilerParams(vmem_limit_bytes=4 * 2**20),
        name="total_rows",
    )(*arrays)


def spread_kernel(chunks, own_ref, other_ref, out_hbm, out_ref, sems):
    tokens, width = out_ref.shape
    capacity = own_ref.shape[0]
    marks = jnp.concatenate([ref[:, width:].astype(jnp.float32) for ref in (own_ref, other_ref)], axis=0)
    lane = lax.broadcasted_iota(jnp.int32, marks.shape, 1)
    number = jnp.sum(jnp.where(lane == 0, marks * 256.0, jnp.where(lane == 1, marks, 0.0)), axis=1, keepdims=True)
    token = lax.broadcasted_iota(jnp.int32, (2 * capacity, tokens), 1).astype(jnp.float32)
    select = jnp.where(token + 1.0 == number, 1.0, 0.0).astype(jnp.bfloat16)
    copies = []
    for i in range(chunks):
        part = slice(i * width // chunks, (i + 1) * width // chunks)
        rows = jnp.concatenate([ref[:, part] for ref in (own_ref, other_ref)], axis=0)
        out_ref[:, part] = lax.dot_general(
            select, rows, (((0,), (0,)), ((), ())), preferred_element_type=jnp.float32
        ).astype(jnp.bfloat16)
        copies.append(pltpu.make_async_copy(out_ref.at[:, part], out_hbm.at[:, part], sems.at[i]))
        copies[-1].start()
    for copy in copies:
        copy.wait()


def spread_rows(own_rows, other_rows, tokens, chunks):
    capacity, wide = own_rows.shape
    width = wide - LANES
    return pl.pallas_call(
        functools.partial(spread_kernel, chunks),
        out_shape=shape_of((tokens, width), jnp.bfloat16),
        in_specs=[VMEM, VMEM],
        out_specs=HBM,
        scratch_shapes=[pltpu.VMEM((tokens, width), jnp.bfloat16), pltpu.SemaphoreType.DMA((chunks,))],
        cost_estimate=cost(4 * capacity * tokens * width, 2 * tokens * width),
        compiler_params=pltpu.CompilerParams(vmem_limit_bytes=16 * 2**20),
        name="spread_rows",
    )(own_rows, other_rows)


def pairwise_shards(block_input, output_grad, expert_ids, gate_weights, gate_proj, up_proj, down_proj):
    tokens = block_input.shape[1]
    width = block_input.shape[2]
    capacity = tokens // 16
    count = 2 * lax.axis_size("dp")
    plane = [offset for offset in range(count) if not offset & 2]
    offsets = plane + [offset | 2 for offset in plane]
    expert_index = lax.axis_index("expert").astype(jnp.int32)
    core_index = lax.axis_index("dp").astype(jnp.int32) & 1
    own = expert_index.reshape(1)
    swapped = (expert_index ^ core_index).reshape(1)
    ids = jnp.transpose(expert_ids, (2, 0, 1))
    weights = jnp.transpose(gate_weights, (2, 0, 1))
    stay = functools.partial(pltpu.with_memory_space_constraint, memory_space=pltpu.HBM)
    *sends, select = pick_rows(
        own, stay(ids), stay(weights), stay(block_input[0]), stay(output_grad[0]), capacity
    )
    upper, lower = stay(up_proj[0, 0]), stay(down_proj[0, 0])
    gate, head = load_weights(stay(gate_proj[0, 0]), upper)
    mine = {0: sends[0]}
    for offset in sorted(plane[1:], reverse=True):
        mine[offset] = swap(sends[offset % 2], offset)
    theirs = {offset: swap(mine[offset], 2) for offset in plane}
    pieces = [mine[offset] for offset in plane] + [theirs[offset] for offset in plane]
    keep, send, scores, delta, hidden = hidden_pass(
        swapped, pieces, offsets, gate, head, upper, lower, capacity
    )
    recv = swap(send, 2)
    chips = count // 4
    *joined, scores = join_cores(keep, scores, recv, chips)
    messages = [send_back(joined[x], x) for x in range(chips)]
    gate_grad, upper_grad, lower_grad = weight_grads(pieces, delta, hidden, width // 2)
    score_rows = {offset: scores[i * capacity : (i + 1) * capacity, :1] for i, offset in enumerate(plane)}
    bit = count // 2
    while bit > 2:
        low = [offset for offset in score_rows if not offset & bit]
        moved = swap(jnp.concatenate([score_rows[offset | bit] for offset in low]), bit)
        score_rows = {
            offset: score_rows[offset] + moved[i * capacity : (i + 1) * capacity]
            for i, offset in enumerate(low)
        }
        bit //= 2
    score_list = [score_rows[0], swap(score_rows[1], 1)]
    weight_grad = score_grads(own, ids, weights, select, score_list, capacity)
    own_rows, other_rows = total_rows(messages)
    received = spread_rows(own_rows, swap(other_rows, 2), tokens, 3)
    return (
        received[None],
        jnp.transpose(weight_grad, (1, 2, 0)),
        gate_grad[None, None],
        upper_grad[None, None],
        lower_grad[None, None],
    )


def shifted(value, axis, steps):
    count = lax.axis_size(axis)
    pairs = [(source, (source + steps) % count) for source in range(count)]
    return lax.ppermute(value, axis, pairs)


def slot_tables(chosen_ids, experts, capacity):
    tok_count, chosen = chosen_ids.shape
    flat_ids = chosen_ids.reshape(-1)
    columns = jnp.arange(experts, dtype=jnp.int32)
    onehot = (flat_ids[:, None] == columns[None, :]).astype(jnp.int32)
    earlier = jnp.cumsum(onehot, axis=0) - onehot
    slot_rank = jnp.sum(earlier * onehot, axis=1)
    kept_pair = (flat_ids < experts) & (slot_rank < capacity)
    slot_index = jnp.where(kept_pair, flat_ids * capacity + slot_rank, experts * capacity)
    slot_rows = jnp.arange(experts * capacity, dtype=jnp.int32)
    placed = slot_index[None, :] == slot_rows[:, None]
    pair_index = jnp.arange(tok_count * chosen, dtype=jnp.int32)
    source_pair = jnp.sum(jnp.where(placed, pair_index[None, :], 0), axis=1)
    filled = jnp.any(placed, axis=1)
    return (slot_index, source_pair, filled)


def general_shards(block_input, output_grad, expert_ids, gate_weights, gate_proj, up_proj, down_proj):
    acts_local = block_input[0]
    grad_local = output_grad[0]
    chosen_ids = expert_ids[0]
    route_weight = gate_weights[0]
    tok_count, chosen = chosen_ids.shape
    width = acts_local.shape[1]
    local_count = gate_proj.shape[1]
    dp_count = lax.axis_size("dp")
    expert_count = lax.axis_size("expert")
    experts = local_count * expert_count
    capacity = tok_count // 16
    slot_index, source_pair, filled = slot_tables(chosen_ids, experts, capacity)
    source_token = source_pair // chosen
    slot_weight = route_weight.reshape(-1)[source_pair]
    send_acts = jnp.where(filled[:, None], acts_local[source_token], jnp.zeros((), jnp.bfloat16))
    scaled = slot_weight[:, None] * grad_local[source_token].astype(jnp.float32)
    send_grad = jnp.where(filled[:, None], scaled, 0.0).astype(jnp.bfloat16)
    send_acts = send_acts.reshape(experts, capacity, width)
    send_grad = send_grad.reshape(experts, capacity, width)
    acts_copies = jnp.broadcast_to(send_acts[None], (dp_count,) + send_acts.shape).reshape(
        dp_count * experts, capacity, width
    )
    grad_copies = jnp.broadcast_to(send_grad[None], (dp_count,) + send_grad.shape).reshape(
        dp_count * experts, capacity, width
    )
    recv_acts, recv_grad = (
        lax.all_to_all(acts_copies, ("dp", "expert"), split_axis=0, concat_axis=1, tiled=True),
        lax.all_to_all(grad_copies, ("dp", "expert"), split_axis=0, concat_axis=1, tiled=True),
    )
    gate_local = gate_proj[0]
    upper_local = up_proj[0]
    lower_local = down_proj[0]
    gate_pre = jnp.einsum("erd,edh->erh", recv_acts, gate_local, preferred_element_type=jnp.float32)
    up_value = jnp.einsum(
        "erd,edh->erh", recv_acts, upper_local, preferred_element_type=jnp.float32
    )
    grad_hidden = jnp.einsum(
        "erd,ehd->erh", recv_grad, lower_local, preferred_element_type=jnp.float32
    )
    sigma_gate = jax.nn.sigmoid(gate_pre)
    swish = gate_pre * sigma_gate
    hidden = swish * up_value
    scores = jnp.sum(hidden * grad_hidden, axis=2)
    lower_grad = jnp.einsum(
        "erh,erd->ehd", hidden.astype(jnp.bfloat16), recv_grad, preferred_element_type=jnp.float32
    ).astype(jnp.bfloat16)
    delta_gate = (
        grad_hidden * up_value * sigma_gate * (1.0 + gate_pre * (1.0 - sigma_gate))
    ).astype(jnp.bfloat16)
    delta_up = (grad_hidden * swish).astype(jnp.bfloat16)
    gate_grad = jnp.einsum(
        "erd,erh->edh", recv_acts, delta_gate, preferred_element_type=jnp.float32
    ).astype(jnp.bfloat16)
    upper_grad = jnp.einsum(
        "erd,erh->edh", recv_acts, delta_up, preferred_element_type=jnp.float32
    ).astype(jnp.bfloat16)
    partial_value = jnp.einsum(
        "erh,edh->erd", delta_gate, gate_local, preferred_element_type=jnp.float32
    ) + jnp.einsum("erh,edh->erd", delta_up, upper_local, preferred_element_type=jnp.float32)
    back_rows, back_scores = (
        lax.all_to_all(partial_value, ("dp", "expert"), split_axis=1, concat_axis=0, tiled=True),
        lax.all_to_all(scores, ("dp", "expert"), split_axis=1, concat_axis=0, tiled=True),
    )
    slot_grad = jnp.sum(back_rows.reshape(dp_count, experts * capacity, width), axis=0).astype(
        jnp.bfloat16
    )
    slot_scores = jnp.sum(back_scores.reshape(dp_count, experts * capacity), axis=0)
    token_rows = jnp.arange(tok_count, dtype=jnp.int32)
    token_map = ((source_token[:, None] == token_rows[None, :]) & filled[:, None]).astype(
        jnp.bfloat16
    )
    input_grad = jnp.einsum(
        "st,sd->td", token_map, slot_grad, preferred_element_type=jnp.float32
    ).astype(jnp.bfloat16)
    padded_scores = jnp.concatenate([slot_scores, jnp.zeros((1,), jnp.float32)])
    weight_grad = (padded_scores[slot_index] / route_weight.reshape(-1)).reshape(tok_count, chosen)
    received = shifted(input_grad, "pipe", -1)
    return (received[None], weight_grad[None], gate_grad[None], upper_grad[None], lower_grad[None])


def solution(mesh):
    in_specs = (
        P("pipe", ("dp", "expert"), None),
        P("pipe", ("dp", "expert"), None),
        P("pipe", ("dp", "expert"), None),
        P("pipe", ("dp", "expert"), None),
        P("pipe", "expert", None, "dp"),
        P("pipe", "expert", None, "dp"),
        P("pipe", "expert", "dp", None),
    )
    out_specs = (
        P("pipe", ("dp", "expert"), None),
        P("pipe", ("dp", "expert"), None),
        P("pipe", "expert", None, "dp"),
        P("pipe", "expert", None, "dp"),
        P("pipe", "expert", "dp", None),
    )
    dp_count, expert_count = mesh.shape["dp"], mesh.shape["expert"]

    def shards(*arrays):
        pairwise = (
            expert_count == 2
            and dp_count * expert_count <= PAIRWISE_MAX
            and dp_count > 1
            and power_of_two(dp_count)
            and arrays[4].shape[1] == 1
        )
        return (pairwise_shards if pairwise else general_shards)(*arrays)

    return jax.shard_map(shards, mesh=mesh, in_specs=in_specs, out_specs=out_specs, check_vma=False)
```

```python
import functools

import jax
import jax.numpy as jnp
from jax import lax
from jax.experimental import pallas as pl
from jax.experimental.pallas import tpu as pltpu
from jax.sharding import PartitionSpec as P


PAIRWISE_MAX = 8
LANES = 128
VMEM = pl.BlockSpec(memory_space=pltpu.VMEM)
HBM = pl.BlockSpec(memory_space=pltpu.HBM)


def shape_of(shape, dtype):
    return jax.ShapeDtypeStruct(shape, dtype)


def cost(flops, bytes_moved):
    return pl.CostEstimate(flops=flops, bytes_accessed=bytes_moved, transcendentals=0)


def power_of_two(number):
    return number > 0 and number & (number - 1) == 0


def swap(value, offset):
    count = lax.axis_size("dp") * lax.axis_size("expert")
    return lax.ppermute(value, ("dp", "expert"), [(i, i ^ offset) for i in range(count)])


def send_back(value, across):
    sections = lax.axis_size("pipe")
    chips = lax.axis_size("dp") // 2
    pairs = []
    for s in range(sections):
        for x in range(chips):
            for core in range(2):
                for expert in range(2):
                    source = (s * chips + x) * 4 + 2 * core + expert
                    target = (((s - 1) % sections) * chips + (x ^ across)) * 4 + 2 * expert + core
                    pairs.append((source, target))
    return lax.ppermute(value, ("pipe", "dp", "expert"), pairs)


def pick_kernel(capacity, index_ref, ids_hbm, weight_hbm, acts_hbm, grad_hbm, *refs):
    outs = refs[:2]
    select_ref, ids_ref, weight_ref, acts_ref, grad_ref, sems = refs[2:]
    copies = [
        pltpu.make_async_copy(source, target, sems.at[i])
        for i, (source, target) in enumerate(
            [(ids_hbm, ids_ref), (weight_hbm, weight_ref), (acts_hbm, acts_ref), (grad_hbm, grad_ref)]
        )
    ]
    for copy in copies:
        copy.start()
    chosen, _, tokens = ids_ref.shape
    width = acts_ref.shape[1]
    rows = 2 * capacity
    row = lax.broadcasted_iota(jnp.int32, (rows, tokens), 0)
    row_expert = (row // capacity) ^ (index_ref[0] & 1)
    before = lax.broadcasted_iota(jnp.int32, (tokens, tokens), 0)
    after = lax.broadcasted_iota(jnp.int32, (tokens, tokens), 1)
    earlier = jnp.where(before < after, 1.0, 0.0).astype(jnp.bfloat16)
    slot = (row % capacity).astype(jnp.float32)
    token = lax.broadcasted_iota(jnp.int32, (rows, tokens), 1).astype(jnp.float32)
    lane = lax.broadcasted_iota(jnp.int32, (rows, LANES), 1)
    taken = jnp.zeros((rows, tokens), jnp.float32)
    scale = jnp.zeros((rows, tokens), jnp.float32)
    copies[0].wait()
    copies[1].wait()
    for k in range(chosen):
        same = ids_ref[k] == row_expert
        taken = jnp.where(same, 1.0, taken)
        scale = jnp.where(same, weight_ref[k], scale)
    rank = jnp.dot(taken.astype(jnp.bfloat16), earlier, preferred_element_type=jnp.float32)
    select = jnp.where(rank == slot, taken, 0.0)
    row_scale = jnp.sum(select * scale, axis=1, keepdims=True)
    number = jnp.sum(select * (token + 1.0), axis=1, keepdims=True)
    high = jnp.floor(number / 256.0)
    marks = jnp.where(lane == 0, high, jnp.where(lane == 1, number - 256.0 * high, 0.0))
    select = select.astype(jnp.bfloat16)
    select_ref[...] = select
    copies[2].wait()
    acts_rows = jnp.dot(select, acts_ref[...], preferred_element_type=jnp.float32)
    copies[3].wait()
    grad_rows = jnp.dot(select, grad_ref[...], preferred_element_type=jnp.float32) * row_scale
    for j in range(2):
        part = slice(j * capacity, (j + 1) * capacity)
        outs[j][:, :width] = jnp.concatenate([acts_rows[part], grad_rows[part]], axis=0).astype(jnp.bfloat16)
        outs[j][:, width:] = jnp.concatenate([marks[part]] * 2, axis=0).astype(jnp.bfloat16)


def pick_rows(index, ids, weights, acts, grads, capacity):
    tokens, width = acts.shape
    group = shape_of((2 * capacity, width + LANES), jnp.bfloat16)
    return pl.pallas_call(
        functools.partial(pick_kernel, capacity),
        out_shape=[group, group, shape_of((2 * capacity, tokens), jnp.bfloat16)],
        in_specs=[pl.BlockSpec(memory_space=pltpu.SMEM)] + [HBM] * 4,
        out_specs=[VMEM] * 3,
        scratch_shapes=[
            pltpu.VMEM(ids.shape, jnp.int32),
            pltpu.VMEM(weights.shape, jnp.float32),
            pltpu.VMEM((tokens, width), jnp.bfloat16),
            pltpu.VMEM((tokens, width), jnp.bfloat16),
            pltpu.SemaphoreType.DMA((4,)),
        ],
        cost_estimate=cost(8 * capacity * tokens * width, 4 * tokens * width),
        compiler_params=pltpu.CompilerParams(vmem_limit_bytes=16 * 2**20),
        name="pick_rows",
    )(index, ids, weights, acts, grads)


def load_kernel(*refs):
    count = len(refs) // 2
    sems = refs[-1]
    copies = [pltpu.make_async_copy(refs[i], refs[count + i], sems.at[i]) for i in range(count)]
    for copy in copies:
        copy.start()
    for copy in copies:
        copy.wait()


def load_weights(*arrays):
    return pl.pallas_call(
        load_kernel,
        out_shape=[shape_of(array.shape, array.dtype) for array in arrays],
        in_specs=[HBM] * len(arrays),
        out_specs=[VMEM] * len(arrays),
        scratch_shapes=[pltpu.SemaphoreType.DMA((len(arrays),))],
        cost_estimate=cost(0, 2 * sum(array.size for array in arrays)),
        compiler_params=pltpu.CompilerParams(vmem_limit_bytes=16 * 2**20),
        name="load_weights",
    )(*arrays)


def weave(value, capacity, upper):
    blank = jnp.zeros((capacity, value.shape[1]), value.dtype)
    parts = []
    for p in range(value.shape[0] // capacity):
        part = value[p * capacity : (p + 1) * capacity]
        parts += [part, blank] if upper else [blank, part]
    return jnp.concatenate(parts, axis=0)


def chain(steps):
    count = [0, 0]
    staged = []
    for unit, weights, turned, left, total in steps:
        staged.append((unit, count[unit] % 2))
        count[unit] += 1
    ahead = 2
    for i in range(len(steps) + ahead):
        if i < len(steps):
            unit, weights, turned, _, _ = steps[i]
            pltpu.matmul_push_rhs(weights(), staging_register=staged[i][1], mxu_index=unit, transpose=turned)
        if i >= ahead:
            _, _, _, left, total = steps[i - ahead]
            pltpu.matmul_acc_lhs(total, left(), load_staged_rhs=staged[i - ahead][1])


def hidden_kernel(capacity, offsets, index_ref, *refs):
    pieces = len(offsets)
    swapped = (index_ref[0] ^ (index_ref[0] >> 1)) & 1
    piece_refs = refs[:pieces]
    gate_ref, upper_ref, lower_ref = refs[pieces : pieces + 3]
    keep_ref, send_ref, delta_ref, hidden_ref = refs[pieces + 3 : pieces + 7]
    score_refs = refs[pieces + 7 :]
    width, units = gate_ref.shape
    rows = pieces * capacity
    half = rows // 2
    tile = units

    def acts(start):
        return jnp.concatenate([ref[:capacity, start : start + tile] for ref in piece_refs], axis=0)

    def grads(start):
        return jnp.concatenate([ref[capacity:, start : start + tile] for ref in piece_refs], axis=0)

    def order(value, wanted):
        lists = [
            jnp.concatenate(
                [value[offsets.index(o) * capacity : (offsets.index(o) + 1) * capacity] for o in chosen], axis=0
            )
            for chosen in wanted
        ]
        return jnp.where(swapped == 1, lists[1], lists[0])

    chips = [4 * x for x in range(pieces // 4)]
    kept = ([x | c for x in chips for c in (0, 2)], [x | c | 1 for x in chips for c in (2, 0)])
    sent = ([x | c | 1 for x in chips for c in (0, 2)], [x | c for x in chips for c in (2, 0)])

    def at(ref, start):
        return lambda: ref[start : start + tile]

    def at_column(ref, start):
        return lambda: ref[:, start : start + tile]

    def forward(first, second):
        steps = []
        for start in range(0, width, tile):
            left = functools.partial(acts, start)
            steps.append((0, at(gate_ref, start), False, left, first))
            steps.append((1, at(upper_ref, start), False, left, second))
        chain(steps)
        return pltpu.matmul_pop(first), pltpu.matmul_pop(second)

    def backward(first, second):
        totals = (first, second)
        chain(
            [
                (i % 2, at_column(lower_ref, start), True, functools.partial(grads, start), totals[i % 2])
                for i, start in enumerate(range(0, width, tile))
            ]
        )
        return pltpu.matmul_pop(first) + pltpu.matmul_pop(second)

    totals = [pltpu.ACC(unit)((rows, tile), jnp.float32) for unit in range(2)]
    gate_pre, up_value = pl.run_scoped(forward, *totals)
    grad_hidden = pl.run_scoped(backward, *totals)
    sigma_gate = jax.nn.sigmoid(gate_pre)
    swish = gate_pre * sigma_gate
    hidden = swish * up_value
    scores = jnp.sum(hidden * grad_hidden, axis=1, keepdims=True)
    delta_gate = grad_hidden * up_value * sigma_gate * (1.0 + gate_pre * (1.0 - sigma_gate))
    delta_up = grad_hidden * swish
    marks = jnp.concatenate([ref[:, width:].astype(jnp.float32)[:capacity] for ref in piece_refs], axis=0)
    gate_part = jnp.concatenate([order(delta_gate, kept), order(delta_gate, sent)]).astype(jnp.bfloat16)
    upper_part = jnp.concatenate([order(delta_up, kept), order(delta_up, sent)]).astype(jnp.bfloat16)
    keep_ref[:, width:] = order(marks, kept)

    def back(*accs):
        starts = list(range(0, width, tile))
        for group in range(0, len(starts), 4):
            steps = []
            for source in range(2):
                for i, start in enumerate(starts[group : group + 4]):
                    unit = i % 2
                    weights = at((gate_ref, upper_ref)[source], start)
                    left = (gate_part, upper_part)[source]
                    total = accs[2 * ((group // 4 * 2 + i // 2) % 2) + unit]
                    steps.append((unit, weights, True, lambda left=left: left, total))
            ordered = [steps[i] for i in (0, 1, 4, 5, 2, 3, 6, 7) if i < len(steps)] if len(steps) == 8 else steps
            chain(ordered)
            for i, start in enumerate(starts[group : group + 4]):
                total = accs[2 * ((group // 4 * 2 + i // 2) % 2) + i % 2]
                block = pltpu.matmul_pop(total)
                keep_ref[:, start : start + tile] = block[:half]
                send_ref[:, start : start + tile] = block[half:].astype(jnp.bfloat16)

    pl.run_scoped(back, *totals, *totals)
    lane = lax.broadcasted_iota(jnp.int32, (capacity, LANES), 1)
    for x, ref in enumerate(score_refs):
        spots = [offsets.index(4 * x + j) * capacity for j in range(4)]
        ref[...] = sum(jnp.where(lane == j, scores[spot : spot + capacity], 0.0) for j, spot in enumerate(spots))
    delta_ref[:, :units] = weave(delta_gate, capacity, True).astype(jnp.bfloat16)
    delta_ref[:, units:] = weave(delta_up, capacity, True).astype(jnp.bfloat16)
    hidden_ref[...] = weave(hidden, capacity, False).astype(jnp.bfloat16)


def hidden_pass(index, pieces, offsets, gate, upper, lower, capacity):
    width, units = gate.shape
    count = len(pieces)
    half = count * capacity // 2
    rows = 2 * count * capacity
    return pl.pallas_call(
        functools.partial(hidden_kernel, capacity, offsets),
        out_shape=[
            shape_of((half, width + LANES), jnp.float32),
            shape_of((half, width), jnp.bfloat16),
            shape_of((rows, 2 * units), jnp.bfloat16),
            shape_of((rows, units), jnp.bfloat16),
        ]
        + [shape_of((capacity, LANES), jnp.float32)] * (count // 4),
        in_specs=[pl.BlockSpec(memory_space=pltpu.SMEM)] + [VMEM] * (count + 3),
        out_specs=[VMEM] * (4 + count // 4),
        cost_estimate=cost(10 * rows * width * units, 6 * width * units),
        compiler_params=pltpu.CompilerParams(vmem_limit_bytes=24 * 2**20),
        name="hidden_pass",
    )(index, *pieces, gate, upper, lower)


def join_kernel(keep_ref, recv_ref, *out_refs):
    width = recv_ref.shape[1]
    for j, ref in enumerate(out_refs):
        rows = ref.shape[0]
        part = slice(j * rows, (j + 1) * rows)
        ref[:, :width] = (keep_ref[part, :width] + recv_ref[part].astype(jnp.float32)).astype(jnp.bfloat16)
        ref[:, width:] = keep_ref[part, width:].astype(jnp.bfloat16)


def join_cores(keep, recv, messages):
    half, wide = keep.shape
    return pl.pallas_call(
        join_kernel,
        out_shape=[shape_of((half // messages, wide), jnp.bfloat16)] * messages,
        in_specs=[VMEM] * 2,
        out_specs=[VMEM] * messages,
        cost_estimate=cost(2 * half * wide, 8 * half * wide),
        compiler_params=pltpu.CompilerParams(vmem_limit_bytes=8 * 2**20),
        name="join_cores",
    )(keep, recv)


def weights_kernel(pieces, chunks, *refs):
    piece_refs = refs[:pieces]
    delta_ref, hidden_ref, *outs = refs[pieces:]
    hbm_refs, buffers, sems = outs[:3], outs[3:6], outs[6]
    width, units = buffers[0].shape
    down = (((0,), (0,)), ((), ()))
    copies = []
    for i in range(chunks):
        part = slice(i * width // chunks, (i + 1) * width // chunks)
        rows = jnp.concatenate([ref[:, part] for ref in piece_refs], axis=0)
        both = lax.dot_general(rows, delta_ref[...], down, preferred_element_type=jnp.float32)
        buffers[0][part] = both[:, :units].astype(jnp.bfloat16)
        buffers[1][part] = both[:, units:].astype(jnp.bfloat16)
        buffers[2][:, part] = lax.dot_general(
            hidden_ref[...], rows, down, preferred_element_type=jnp.float32
        ).astype(jnp.bfloat16)
        for j, spot in enumerate(((part,), (part,), (slice(None), part))):
            copy = pltpu.make_async_copy(buffers[j].at[spot], hbm_refs[j].at[spot], sems.at[j, i])
            copy.start()
            copies.append(copy)
    for copy in copies:
        copy.wait()


def weight_grads(pieces, delta, hidden, chunks):
    width = pieces[0].shape[1] - LANES
    rows, units = hidden.shape
    count = len(pieces)
    shapes = [(width, units), (width, units), (units, width)]
    return pl.pallas_call(
        functools.partial(weights_kernel, count, chunks),
        out_shape=[shape_of(shape, jnp.bfloat16) for shape in shapes],
        in_specs=[VMEM] * (count + 2),
        out_specs=[HBM] * 3,
        scratch_shapes=[pltpu.VMEM(shape, jnp.bfloat16) for shape in shapes]
        + [pltpu.SemaphoreType.DMA((3, chunks))],
        cost_estimate=cost(6 * rows * width * units, 6 * width * units),
        compiler_params=pltpu.CompilerParams(vmem_limit_bytes=24 * 2**20),
        name="weight_grads",
    )(*pieces, delta, hidden)


def add_kernel(left_ref, right_ref, out_ref):
    out_ref[...] = left_ref[...] + right_ref[...]


def add_scores(left, right):
    return pl.pallas_call(
        add_kernel,
        out_shape=shape_of(left.shape, jnp.float32),
        in_specs=[VMEM] * 2,
        out_specs=VMEM,
        cost_estimate=cost(left.size, 12 * left.size),
        compiler_params=pltpu.CompilerParams(vmem_limit_bytes=2**20),
        name="add_scores",
    )(left, right)


def score_kernel(capacity, index_ref, ids_ref, weight_ref, select_ref, near_ref, core_ref, other_ref, out_ref):
    chosen, _, tokens = ids_ref.shape
    scores = (near_ref[:, 0:1] + core_ref[:, 2:3], other_ref[:, 1:2])
    sums = []
    for j in range(2):
        picked = select_ref[j * capacity : (j + 1) * capacity].astype(jnp.float32) * scores[j]
        sums.append(jnp.sum(picked, axis=0, keepdims=True))
    for k in range(chosen):
        value = jnp.zeros((1, tokens), jnp.float32)
        for j in range(2):
            value = jnp.where(ids_ref[k] == ((index_ref[0] & 1) ^ j), sums[j], value)
        out_ref[k] = value / weight_ref[k]


def score_grads(index, ids, weights, select, near, core, other, capacity):
    return pl.pallas_call(
        functools.partial(score_kernel, capacity),
        out_shape=shape_of(weights.shape, jnp.float32),
        in_specs=[pl.BlockSpec(memory_space=pltpu.SMEM)] + [VMEM] * 6,
        out_specs=VMEM,
        cost_estimate=cost(1000, 1000),
        compiler_params=pltpu.CompilerParams(vmem_limit_bytes=4 * 2**20),
        name="score_grads",
    )(index, ids, weights, select, near, core, other)


def total_kernel(messages, *refs):
    own_ref, other_ref = refs[messages:]
    capacity, wide = own_ref.shape
    width = wide - LANES
    total = refs[0][:, :width].astype(jnp.float32)
    for ref in refs[1:messages]:
        total = total + ref[:, :width].astype(jnp.float32)
    marks = refs[0][:, width:].astype(jnp.float32)
    own_ref[:, :width] = total[:capacity].astype(jnp.bfloat16)
    own_ref[:, width:] = marks[:capacity].astype(jnp.bfloat16)
    other_ref[:, :width] = total[capacity:].astype(jnp.bfloat16)
    other_ref[:, width:] = marks[capacity:].astype(jnp.bfloat16)


def total_rows(arrays):
    rows, wide = arrays[0].shape
    return pl.pallas_call(
        functools.partial(total_kernel, len(arrays)),
        out_shape=[shape_of((rows // 2, wide), jnp.bfloat16)] * 2,
        in_specs=[VMEM] * len(arrays),
        out_specs=[VMEM] * 2,
        cost_estimate=cost(rows * wide, 4 * rows * wide),
        compiler_params=pltpu.CompilerParams(vmem_limit_bytes=4 * 2**20),
        name="total_rows",
    )(*arrays)


def spread_kernel(chunks, own_ref, other_ref, out_hbm, out_ref, sems):
    tokens, width = out_ref.shape
    capacity = own_ref.shape[0]
    marks = jnp.concatenate([ref[:, width:].astype(jnp.float32) for ref in (own_ref, other_ref)], axis=0)
    lane = lax.broadcasted_iota(jnp.int32, marks.shape, 1)
    number = jnp.sum(jnp.where(lane == 0, marks * 256.0, jnp.where(lane == 1, marks, 0.0)), axis=1, keepdims=True)
    token = lax.broadcasted_iota(jnp.int32, (2 * capacity, tokens), 1).astype(jnp.float32)
    select = jnp.where(token + 1.0 == number, 1.0, 0.0).astype(jnp.bfloat16)
    copies = []
    for i in range(chunks):
        part = slice(i * width // chunks, (i + 1) * width // chunks)
        rows = jnp.concatenate([ref[:, part] for ref in (own_ref, other_ref)], axis=0)
        out_ref[:, part] = lax.dot_general(
            select, rows, (((0,), (0,)), ((), ())), preferred_element_type=jnp.float32
        ).astype(jnp.bfloat16)
        copies.append(pltpu.make_async_copy(out_ref.at[:, part], out_hbm.at[:, part], sems.at[i]))
        copies[-1].start()
    for copy in copies:
        copy.wait()


def spread_rows(own_rows, other_rows, tokens, chunks):
    capacity, wide = own_rows.shape
    width = wide - LANES
    return pl.pallas_call(
        functools.partial(spread_kernel, chunks),
        out_shape=shape_of((tokens, width), jnp.bfloat16),
        in_specs=[VMEM, VMEM],
        out_specs=HBM,
        scratch_shapes=[pltpu.VMEM((tokens, width), jnp.bfloat16), pltpu.SemaphoreType.DMA((chunks,))],
        cost_estimate=cost(4 * capacity * tokens * width, 2 * tokens * width),
        compiler_params=pltpu.CompilerParams(vmem_limit_bytes=16 * 2**20),
        name="spread_rows",
    )(own_rows, other_rows)


def pairwise_shards(block_input, output_grad, expert_ids, gate_weights, gate_proj, up_proj, down_proj):
    tokens = block_input.shape[1]
    capacity = tokens // 16
    count = 2 * lax.axis_size("dp")
    plane = [offset for offset in range(count) if not offset & 2]
    offsets = plane + [offset | 2 for offset in plane]
    index = lax.axis_index(("dp", "expert")).astype(jnp.int32).reshape(1)
    ids = jnp.transpose(expert_ids, (2, 0, 1))
    weights = jnp.transpose(gate_weights, (2, 0, 1))
    stay = functools.partial(pltpu.with_memory_space_constraint, memory_space=pltpu.HBM)
    *sends, select = pick_rows(index, stay(ids), stay(weights), stay(block_input[0]), stay(output_grad[0]), capacity)
    gate, upper, lower = load_weights(*[stay(array[0, 0]) for array in (gate_proj, up_proj, down_proj)])
    mine = {0: sends[0]}
    for offset in sorted(plane[1:], reverse=True):
        mine[offset] = swap(sends[offset % 2], offset)
    theirs = {offset: swap(mine[offset], 2) for offset in plane}
    pieces = [mine[offset] for offset in plane] + [theirs[offset] for offset in plane]
    keep, send, delta, hidden, near, *far = hidden_pass(
        index, pieces, offsets, gate, upper, lower, capacity
    )
    recv = swap(send, 2)
    for scores in far:
        moved = swap(scores, 4)
        near = add_scores(near, moved)
    chips = count // 4
    joined = join_cores(keep, recv, chips)
    messages = [send_back(joined[x], x) for x in range(chips)]
    gate_grad, upper_grad, lower_grad = weight_grads(pieces, delta, hidden, 6)
    core = swap(near, 2)
    other = swap(near[:, :2] + core[:, 2:4], 1)
    weight_grad = score_grads(index, ids, weights, select, near, core, other, capacity)
    own_rows, other_rows = total_rows(messages)
    received = spread_rows(own_rows, swap(other_rows, 2), tokens, 3)
    return (
        received[None],
        jnp.transpose(weight_grad, (1, 2, 0)),
        gate_grad[None, None],
        upper_grad[None, None],
        lower_grad[None, None],
    )


def shifted(value, axis, steps):
    count = lax.axis_size(axis)
    pairs = [(source, (source + steps) % count) for source in range(count)]
    return lax.ppermute(value, axis, pairs)


def slot_tables(chosen_ids, experts, capacity):
    tok_count, chosen = chosen_ids.shape
    flat_ids = chosen_ids.reshape(-1)
    columns = jnp.arange(experts, dtype=jnp.int32)
    onehot = (flat_ids[:, None] == columns[None, :]).astype(jnp.int32)
    earlier = jnp.cumsum(onehot, axis=0) - onehot
    slot_rank = jnp.sum(earlier * onehot, axis=1)
    kept_pair = (flat_ids < experts) & (slot_rank < capacity)
    slot_index = jnp.where(kept_pair, flat_ids * capacity + slot_rank, experts * capacity)
    slot_rows = jnp.arange(experts * capacity, dtype=jnp.int32)
    placed = slot_index[None, :] == slot_rows[:, None]
    pair_index = jnp.arange(tok_count * chosen, dtype=jnp.int32)
    source_pair = jnp.sum(jnp.where(placed, pair_index[None, :], 0), axis=1)
    filled = jnp.any(placed, axis=1)
    return (slot_index, source_pair, filled)


def general_shards(block_input, output_grad, expert_ids, gate_weights, gate_proj, up_proj, down_proj):
    acts_local = block_input[0]
    grad_local = output_grad[0]
    chosen_ids = expert_ids[0]
    route_weight = gate_weights[0]
    tok_count, chosen = chosen_ids.shape
    width = acts_local.shape[1]
    local_count = gate_proj.shape[1]
    dp_count = lax.axis_size("dp")
    expert_count = lax.axis_size("expert")
    experts = local_count * expert_count
    capacity = tok_count // 16
    slot_index, source_pair, filled = slot_tables(chosen_ids, experts, capacity)
    source_token = source_pair // chosen
    slot_weight = route_weight.reshape(-1)[source_pair]
    send_acts = jnp.where(filled[:, None], acts_local[source_token], jnp.zeros((), jnp.bfloat16))
    scaled = slot_weight[:, None] * grad_local[source_token].astype(jnp.float32)
    send_grad = jnp.where(filled[:, None], scaled, 0.0).astype(jnp.bfloat16)
    send_acts = send_acts.reshape(experts, capacity, width)
    send_grad = send_grad.reshape(experts, capacity, width)
    acts_copies = jnp.broadcast_to(send_acts[None], (dp_count,) + send_acts.shape).reshape(
        dp_count * experts, capacity, width
    )
    grad_copies = jnp.broadcast_to(send_grad[None], (dp_count,) + send_grad.shape).reshape(
        dp_count * experts, capacity, width
    )
    recv_acts, recv_grad = (
        lax.all_to_all(acts_copies, ("dp", "expert"), split_axis=0, concat_axis=1, tiled=True),
        lax.all_to_all(grad_copies, ("dp", "expert"), split_axis=0, concat_axis=1, tiled=True),
    )
    gate_local = gate_proj[0]
    upper_local = up_proj[0]
    lower_local = down_proj[0]
    gate_pre = jnp.einsum("erd,edh->erh", recv_acts, gate_local, preferred_element_type=jnp.float32)
    up_value = jnp.einsum(
        "erd,edh->erh", recv_acts, upper_local, preferred_element_type=jnp.float32
    )
    grad_hidden = jnp.einsum(
        "erd,ehd->erh", recv_grad, lower_local, preferred_element_type=jnp.float32
    )
    sigma_gate = jax.nn.sigmoid(gate_pre)
    swish = gate_pre * sigma_gate
    hidden = swish * up_value
    scores = jnp.sum(hidden * grad_hidden, axis=2)
    lower_grad = jnp.einsum(
        "erh,erd->ehd", hidden.astype(jnp.bfloat16), recv_grad, preferred_element_type=jnp.float32
    ).astype(jnp.bfloat16)
    delta_gate = (
        grad_hidden * up_value * sigma_gate * (1.0 + gate_pre * (1.0 - sigma_gate))
    ).astype(jnp.bfloat16)
    delta_up = (grad_hidden * swish).astype(jnp.bfloat16)
    gate_grad = jnp.einsum(
        "erd,erh->edh", recv_acts, delta_gate, preferred_element_type=jnp.float32
    ).astype(jnp.bfloat16)
    upper_grad = jnp.einsum(
        "erd,erh->edh", recv_acts, delta_up, preferred_element_type=jnp.float32
    ).astype(jnp.bfloat16)
    partial_value = jnp.einsum(
        "erh,edh->erd", delta_gate, gate_local, preferred_element_type=jnp.float32
    ) + jnp.einsum("erh,edh->erd", delta_up, upper_local, preferred_element_type=jnp.float32)
    back_rows, back_scores = (
        lax.all_to_all(partial_value, ("dp", "expert"), split_axis=1, concat_axis=0, tiled=True),
        lax.all_to_all(scores, ("dp", "expert"), split_axis=1, concat_axis=0, tiled=True),
    )
    slot_grad = jnp.sum(back_rows.reshape(dp_count, experts * capacity, width), axis=0).astype(
        jnp.bfloat16
    )
    slot_scores = jnp.sum(back_scores.reshape(dp_count, experts * capacity), axis=0)
    token_rows = jnp.arange(tok_count, dtype=jnp.int32)
    token_map = ((source_token[:, None] == token_rows[None, :]) & filled[:, None]).astype(
        jnp.bfloat16
    )
    input_grad = jnp.einsum(
        "st,sd->td", token_map, slot_grad, preferred_element_type=jnp.float32
    ).astype(jnp.bfloat16)
    padded_scores = jnp.concatenate([slot_scores, jnp.zeros((1,), jnp.float32)])
    weight_grad = (padded_scores[slot_index] / route_weight.reshape(-1)).reshape(tok_count, chosen)
    received = shifted(input_grad, "pipe", -1)
    return (received[None], weight_grad[None], gate_grad[None], upper_grad[None], lower_grad[None])


def solution(mesh):
    in_specs = (
        P("pipe", ("dp", "expert"), None),
        P("pipe", ("dp", "expert"), None),
        P("pipe", ("dp", "expert"), None),
        P("pipe", ("dp", "expert"), None),
        P("pipe", "expert", None, "dp"),
        P("pipe", "expert", None, "dp"),
        P("pipe", "expert", "dp", None),
    )
    out_specs = (
        P("pipe", ("dp", "expert"), None),
        P("pipe", ("dp", "expert"), None),
        P("pipe", "expert", None, "dp"),
        P("pipe", "expert", None, "dp"),
        P("pipe", "expert", "dp", None),
    )
    dp_count, expert_count = mesh.shape["dp"], mesh.shape["expert"]

    def shards(*arrays):
        pairwise = (
            expert_count == 2
            and dp_count * expert_count <= PAIRWISE_MAX
            and dp_count > 1
            and power_of_two(dp_count)
            and arrays[4].shape[1] == 1
        )
        return (pairwise_shards if pairwise else general_shards)(*arrays)

    return jax.shard_map(shards, mesh=mesh, in_specs=in_specs, out_specs=out_specs, check_vma=False)
```

```python
import functools

import jax
import jax.numpy as jnp
from jax import lax
from jax.experimental import pallas as pl
from jax.experimental.pallas import tpu as pltpu
from jax.sharding import PartitionSpec as P


PAIRWISE_MAX = 8
LANES = 128
VMEM = pl.BlockSpec(memory_space=pltpu.VMEM)
HBM = pl.BlockSpec(memory_space=pltpu.HBM)


def shape_of(shape, dtype):
    return jax.ShapeDtypeStruct(shape, dtype)


def cost(flops, bytes_moved):
    return pl.CostEstimate(flops=flops, bytes_accessed=bytes_moved, transcendentals=0)


def power_of_two(number):
    return number > 0 and number & (number - 1) == 0


def swap(value, offset):
    count = lax.axis_size("dp") * lax.axis_size("expert")
    return lax.ppermute(value, ("dp", "expert"), [(i, i ^ offset) for i in range(count)])


def send_back(value, across, flip):
    sections = lax.axis_size("pipe")
    chips = lax.axis_size("dp") // 2
    pairs = []
    for s in range(sections):
        for x in range(chips):
            for core in range(2):
                for expert in range(2):
                    source = (s * chips + x) * 4 + 2 * core + expert
                    target = (((s - 1) % sections) * chips + (x ^ across)) * 4 + 2 * (expert ^ flip) + core
                    pairs.append((source, target))
    return lax.ppermute(value, ("pipe", "dp", "expert"), pairs)


def pick_kernel(capacity, index_ref, ids_hbm, weight_hbm, acts_hbm, grad_hbm, *refs):
    outs = refs[:2]
    select_ref, ids_ref, weight_ref, acts_ref, grad_ref, sems = refs[2:]
    copies = [
        pltpu.make_async_copy(source, target, sems.at[i])
        for i, (source, target) in enumerate(
            [(ids_hbm, ids_ref), (weight_hbm, weight_ref), (acts_hbm, acts_ref), (grad_hbm, grad_ref)]
        )
    ]
    for copy in copies:
        copy.start()
    chosen, _, tokens = ids_ref.shape
    width = acts_ref.shape[1]
    rows = 2 * capacity
    row = lax.broadcasted_iota(jnp.int32, (rows, tokens), 0)
    row_expert = (row // capacity) ^ (index_ref[0] & 1)
    before = lax.broadcasted_iota(jnp.int32, (tokens, tokens), 0)
    after = lax.broadcasted_iota(jnp.int32, (tokens, tokens), 1)
    earlier = jnp.where(before < after, 1.0, 0.0).astype(jnp.bfloat16)
    slot = (row % capacity).astype(jnp.float32)
    token = lax.broadcasted_iota(jnp.int32, (rows, tokens), 1).astype(jnp.float32)
    lane = lax.broadcasted_iota(jnp.int32, (rows, LANES), 1)
    taken = jnp.zeros((rows, tokens), jnp.float32)
    scale = jnp.zeros((rows, tokens), jnp.float32)
    copies[0].wait()
    copies[1].wait()
    for k in range(chosen):
        same = ids_ref[k] == row_expert
        taken = jnp.where(same, 1.0, taken)
        scale = jnp.where(same, weight_ref[k], scale)
    rank = jnp.dot(taken.astype(jnp.bfloat16), earlier, preferred_element_type=jnp.float32)
    select = jnp.where(rank == slot, taken, 0.0)
    row_scale = jnp.sum(select * scale, axis=1, keepdims=True)
    number = jnp.sum(select * (token + 1.0), axis=1, keepdims=True)
    high = jnp.floor(number / 256.0)
    marks = jnp.where(lane == 0, high, jnp.where(lane == 1, number - 256.0 * high, 0.0))
    select = select.astype(jnp.bfloat16)
    select_ref[...] = select
    copies[2].wait()
    acts_rows = jnp.dot(select, acts_ref[...], preferred_element_type=jnp.float32)
    copies[3].wait()
    grad_rows = jnp.dot(select, grad_ref[...], preferred_element_type=jnp.float32) * row_scale
    for j in range(2):
        part = slice(j * capacity, (j + 1) * capacity)
        outs[j][:, :width] = jnp.concatenate([acts_rows[part], grad_rows[part]], axis=0).astype(jnp.bfloat16)
        outs[j][:, width:] = jnp.concatenate([marks[part]] * 2, axis=0).astype(jnp.bfloat16)


def pick_rows(index, ids, weights, acts, grads, capacity):
    tokens, width = acts.shape
    group = shape_of((2 * capacity, width + LANES), jnp.bfloat16)
    return pl.pallas_call(
        functools.partial(pick_kernel, capacity),
        out_shape=[
            group,
            group,
            shape_of((2 * capacity, tokens), jnp.bfloat16),
            shape_of(ids.shape, jnp.int32),
            shape_of(weights.shape, jnp.float32),
        ],
        in_specs=[pl.BlockSpec(memory_space=pltpu.SMEM)] + [HBM] * 4,
        out_specs=[VMEM] * 5,
        scratch_shapes=[
            pltpu.VMEM((tokens, width), jnp.bfloat16),
            pltpu.VMEM((tokens, width), jnp.bfloat16),
            pltpu.SemaphoreType.DMA((4,)),
        ],
        cost_estimate=cost(8 * capacity * tokens * width, 4 * tokens * width),
        compiler_params=pltpu.CompilerParams(vmem_limit_bytes=16 * 2**20),
        name="pick_rows",
    )(index, ids, weights, acts, grads)


def load_kernel(*refs):
    count = len(refs) // 2
    sems = refs[-1]
    copies = [pltpu.make_async_copy(refs[i], refs[count + i], sems.at[i]) for i in range(count)]
    for copy in copies:
        copy.start()
    for copy in copies:
        copy.wait()


def load_weights(*arrays):
    return pl.pallas_call(
        load_kernel,
        out_shape=[shape_of(array.shape, array.dtype) for array in arrays],
        in_specs=[HBM] * len(arrays),
        out_specs=[VMEM] * len(arrays),
        scratch_shapes=[pltpu.SemaphoreType.DMA((len(arrays),))],
        cost_estimate=cost(0, 2 * sum(array.size for array in arrays)),
        compiler_params=pltpu.CompilerParams(vmem_limit_bytes=16 * 2**20),
        name="load_weights",
    )(*arrays)


def weave(value, capacity, upper):
    blank = jnp.zeros((capacity, value.shape[1]), value.dtype)
    parts = []
    for p in range(value.shape[0] // capacity):
        part = value[p * capacity : (p + 1) * capacity]
        parts += [part, blank] if upper else [blank, part]
    return jnp.concatenate(parts, axis=0)


def chain(steps):
    count = [0, 0]
    staged = []
    for unit, *_ in steps:
        staged.append(count[unit] % 2)
        count[unit] += 1
    ahead = 2
    for i in range(len(steps) + ahead):
        if i < len(steps):
            unit, weights, turned = steps[i][:3]
            pltpu.matmul_push_rhs(weights(), staging_register=staged[i], mxu_index=unit, transpose=turned)
        if i >= ahead:
            left, total, after = steps[i - ahead][3:]
            pltpu.matmul_acc_lhs(total, left(), load_staged_rhs=staged[i - ahead])
            if after is not None:
                after()


def hidden_kernel(capacity, offsets, index_ref, *refs):
    pieces = len(offsets)
    swapped = (index_ref[0] ^ (index_ref[0] >> 1)) & 1
    piece_refs = refs[:pieces]
    gate_ref, upper_ref, lower_ref = refs[pieces : pieces + 3]
    keep_ref, send_ref, delta_ref, hidden_ref = refs[pieces + 3 : pieces + 7]
    score_refs = refs[pieces + 7 :]
    width, units = gate_ref.shape
    rows = pieces * capacity
    half = rows // 2
    tile = units

    def acts(start):
        return jnp.concatenate([ref[:capacity, start : start + tile] for ref in piece_refs], axis=0)

    def grads(start):
        return jnp.concatenate([ref[capacity:, start : start + tile] for ref in piece_refs], axis=0)

    def order(value, wanted):
        lists = [
            jnp.concatenate(
                [value[offsets.index(o) * capacity : (offsets.index(o) + 1) * capacity] for o in chosen], axis=0
            )
            for chosen in wanted
        ]
        return jnp.where(swapped == 1, lists[1], lists[0])

    chips = [4 * x for x in range(pieces // 4)]
    kept = ([x | c for x in chips for c in (0, 2)], [x | c | 1 for x in chips for c in (2, 0)])
    sent = ([x | c | 1 for x in chips for c in (0, 2)], [x | c for x in chips for c in (2, 0)])

    def at(ref, start):
        return lambda: ref[start : start + tile]

    def at_column(ref, start):
        return lambda: ref[:, start : start + tile]

    def forward(first, second, third, fourth):
        taken = []

        def take():
            taken.extend((pltpu.matmul_pop(first), pltpu.matmul_pop(second)))

        steps = []
        for start in range(0, width, tile):
            left = functools.partial(acts, start)
            steps.append((0, at(gate_ref, start), False, left, first, None))
            steps.append((1, at(upper_ref, start), False, left, second, None))
        for i, start in enumerate(range(0, width, tile)):
            left = functools.partial(grads, start)
            total = (third, fourth)[i % 2]
            steps.append((i % 2, at_column(lower_ref, start), True, left, total, take if i == 1 else None))
        chain(steps)
        return (*taken, pltpu.matmul_pop(third) + pltpu.matmul_pop(fourth))

    totals = [pltpu.ACC(unit)((rows, tile), jnp.float32) for unit in range(2)]
    gate_pre, up_value, grad_hidden = pl.run_scoped(forward, *totals, *totals)
    sigma_gate = jax.nn.sigmoid(gate_pre)
    swish = gate_pre * sigma_gate
    hidden = swish * up_value
    scores = jnp.sum(hidden * grad_hidden, axis=1, keepdims=True)
    delta_gate = grad_hidden * up_value * sigma_gate * (1.0 + gate_pre * (1.0 - sigma_gate))
    delta_up = grad_hidden * swish
    marks = jnp.concatenate([ref[:, width:].astype(jnp.float32)[:capacity] for ref in piece_refs], axis=0)
    gate_part = jnp.concatenate([order(delta_gate, kept), order(delta_gate, sent)]).astype(jnp.bfloat16)
    upper_part = jnp.concatenate([order(delta_up, kept), order(delta_up, sent)]).astype(jnp.bfloat16)
    keep_ref[:, width:] = order(marks, kept)

    def back(*accs):
        starts = list(range(0, width, tile))

        def store(i):
            block = pltpu.matmul_pop(accs[i % len(accs)])
            keep_ref[:, starts[i] : starts[i] + tile] = block[:half]
            send_ref[:, starts[i] : starts[i] + tile] = block[half:].astype(jnp.bfloat16)

        steps = []
        for pair in range(0, len(starts), 2):
            for source in range(2):
                for i in range(pair, min(pair + 2, len(starts))):
                    weights = at((gate_ref, upper_ref)[source], starts[i])
                    left = (gate_part, upper_part)[source]
                    after = functools.partial(store, i - 2) if source == 0 and i >= 2 else None
                    steps.append((i % 2, weights, True, lambda left=left: left, accs[i % len(accs)], after))
        chain(steps)
        for i in range(max(0, len(starts) - 2), len(starts)):
            store(i)

    pl.run_scoped(back, *totals, *totals)
    lane = lax.broadcasted_iota(jnp.int32, (capacity, LANES), 1)
    for x, ref in enumerate(score_refs):
        spots = [offsets.index(4 * x + j) * capacity for j in range(4)]
        ref[...] = sum(jnp.where(lane == j, scores[spot : spot + capacity], 0.0) for j, spot in enumerate(spots))
    delta_ref[:, :units] = weave(delta_gate, capacity, True).astype(jnp.bfloat16)
    delta_ref[:, units:] = weave(delta_up, capacity, True).astype(jnp.bfloat16)
    hidden_ref[...] = weave(hidden, capacity, False).astype(jnp.bfloat16)


def hidden_pass(index, pieces, offsets, gate, upper, lower, capacity):
    width, units = gate.shape
    count = len(pieces)
    half = count * capacity // 2
    rows = 2 * count * capacity
    return pl.pallas_call(
        functools.partial(hidden_kernel, capacity, offsets),
        out_shape=[
            shape_of((half, width + LANES), jnp.float32),
            shape_of((half, width), jnp.bfloat16),
            shape_of((rows, 2 * units), jnp.bfloat16),
            shape_of((rows, units), jnp.bfloat16),
        ]
        + [shape_of((capacity, LANES), jnp.float32)] * (count // 4),
        in_specs=[pl.BlockSpec(memory_space=pltpu.SMEM)] + [VMEM] * (count + 3),
        out_specs=[VMEM] * (4 + count // 4),
        cost_estimate=cost(10 * rows * width * units, 6 * width * units),
        compiler_params=pltpu.CompilerParams(vmem_limit_bytes=24 * 2**20),
        name="hidden_pass",
    )(index, *pieces, gate, upper, lower)


def join_kernel(keep_ref, recv_ref, *out_refs):
    width = recv_ref.shape[1]
    start = 0
    for ref in out_refs:
        part = slice(start, start + ref.shape[0])
        ref[:, :width] = (keep_ref[part, :width] + recv_ref[part].astype(jnp.float32)).astype(jnp.bfloat16)
        ref[:, width:] = keep_ref[part, width:].astype(jnp.bfloat16)
        start += ref.shape[0]


def join_cores(keep, recv, capacity):
    half, wide = keep.shape
    sizes = [capacity, capacity] + [half - 2 * capacity] * (half > 2 * capacity)
    return pl.pallas_call(
        join_kernel,
        out_shape=[shape_of((size, wide), jnp.bfloat16) for size in sizes],
        in_specs=[VMEM] * 2,
        out_specs=[VMEM] * len(sizes),
        cost_estimate=cost(2 * half * wide, 8 * half * wide),
        compiler_params=pltpu.CompilerParams(vmem_limit_bytes=8 * 2**20),
        name="join_cores",
    )(keep, recv)


def weights_kernel(pieces, chunks, chosen, *refs):
    piece_refs = refs[:pieces]
    delta_ref, hidden_ref = refs[pieces : pieces + 2]
    hbm_refs, buffers, sems = refs[-7:-4], refs[-4:-1], refs[-1]
    width, units = buffers[0].shape
    down = (((0,), (0,)), ((), ()))

    @pl.when(chosen(lax.axis_index("pipe"), lax.axis_size("pipe")))
    def _():
        copies = []
        for i in range(chunks):
            part = slice(i * width // chunks, (i + 1) * width // chunks)
            rows = jnp.concatenate([ref[:, part] for ref in piece_refs], axis=0)
            both = lax.dot_general(rows, delta_ref[...], down, preferred_element_type=jnp.float32)
            buffers[0][part] = both[:, :units].astype(jnp.bfloat16)
            buffers[1][part] = both[:, units:].astype(jnp.bfloat16)
            buffers[2][:, part] = lax.dot_general(
                hidden_ref[...], rows, down, preferred_element_type=jnp.float32
            ).astype(jnp.bfloat16)
            for j, spot in enumerate(((part,), (part,), (slice(None), part))):
                copy = pltpu.make_async_copy(buffers[j].at[spot], hbm_refs[j].at[spot], sems.at[j, i])
                copy.start()
                copies.append(copy)
        for copy in copies:
            copy.wait()


def weight_grads(chosen, pieces, delta, hidden, earlier, chunks):
    width = pieces[0].shape[1] - LANES
    rows, units = hidden.shape
    count = len(pieces)
    shapes = [(width, units), (width, units), (units, width)]
    return pl.pallas_call(
        functools.partial(weights_kernel, count, chunks, chosen),
        out_shape=[shape_of(shape, jnp.bfloat16) for shape in shapes],
        in_specs=[VMEM] * (count + 2) + [HBM] * len(earlier),
        out_specs=[HBM] * 3,
        input_output_aliases={2 + count + j: j for j in range(len(earlier))},
        scratch_shapes=[pltpu.VMEM(shape, jnp.bfloat16) for shape in shapes]
        + [pltpu.SemaphoreType.DMA((3, chunks))],
        cost_estimate=cost(6 * rows * width * units, 6 * width * units),
        compiler_params=pltpu.CompilerParams(vmem_limit_bytes=24 * 2**20),
        name="weight_grads",
    )(*pieces, delta, hidden, *earlier)


def is_first(section, sections):
    return section == 0


def is_last(section, sections):
    return (section == sections - 1) & (section != 0)


def is_between(section, sections):
    return (section != sections - 1) & (section != 0)


def cut_kernel(rows_ref, out_ref):
    out_ref[...] = rows_ref[out_ref.shape[0] :]


def lower_half(rows):
    count, wide = rows.shape
    return pl.pallas_call(
        cut_kernel,
        out_shape=shape_of((count // 2, wide), rows.dtype),
        in_specs=[VMEM],
        out_specs=VMEM,
        cost_estimate=cost(0, 4 * rows.size),
        compiler_params=pltpu.CompilerParams(vmem_limit_bytes=2 * 2**20),
        name="lower_half",
    )(rows)


def add_kernel(left_ref, right_ref, out_ref):
    out_ref[...] = left_ref[...] + right_ref[...]


def add_scores(left, right):
    return pl.pallas_call(
        add_kernel,
        out_shape=shape_of(left.shape, jnp.float32),
        in_specs=[VMEM] * 2,
        out_specs=VMEM,
        cost_estimate=cost(left.size, 12 * left.size),
        compiler_params=pltpu.CompilerParams(vmem_limit_bytes=2**20),
        name="add_scores",
    )(left, right)


def spread_kernel(chunks, terms, *refs):
    own_refs, other_refs = refs[:terms], refs[terms : 2 * terms]
    ids_ref, weight_ref, select_ref, near_ref, core_ref, side_ref, corner_ref = refs[2 * terms : 2 * terms + 7]
    out_hbm, score_hbm, out_ref, score_ref, sems = refs[2 * terms + 7 :]
    tokens, width = out_ref.shape
    capacity = other_refs[0].shape[0]
    marks = jnp.concatenate(
        [group[0][:capacity, width:].astype(jnp.float32) for group in (own_refs, other_refs)], axis=0
    )
    lane = lax.broadcasted_iota(jnp.int32, marks.shape, 1)
    number = jnp.sum(jnp.where(lane == 0, marks * 256.0, jnp.where(lane == 1, marks, 0.0)), axis=1, keepdims=True)
    token = lax.broadcasted_iota(jnp.int32, (2 * capacity, tokens), 1).astype(jnp.float32)
    select = jnp.where(token + 1.0 == number, 1.0, 0.0).astype(jnp.bfloat16)
    copies = []
    for i in range(chunks):
        part = slice(i * width // chunks, (i + 1) * width // chunks)
        rows = jnp.concatenate(
            [
                sum(ref[:capacity, part].astype(jnp.float32) for ref in group)
                for group in (own_refs, other_refs)
            ],
            axis=0,
        )
        out_ref[:, part] = lax.dot_general(
            select, rows.astype(jnp.bfloat16), (((0,), (0,)), ((), ())), preferred_element_type=jnp.float32
        ).astype(jnp.bfloat16)
        copies.append(pltpu.make_async_copy(out_ref.at[:, part], out_hbm.at[:, part], sems.at[i]))
        copies[-1].start()
    own = lax.axis_index("expert")
    scores = (near_ref[:, 0:1] + core_ref[:, 2:3], side_ref[:, 1:2] + corner_ref[:, 3:4])
    sums = []
    for j in range(2):
        picked = select_ref[j * capacity : (j + 1) * capacity].astype(jnp.float32) * scores[j]
        sums.append(jnp.sum(picked, axis=0, keepdims=True))
    for k in range(ids_ref.shape[0]):
        value = jnp.zeros((1, tokens), jnp.float32)
        for j in range(2):
            value = jnp.where(ids_ref[k] == (own ^ j), sums[j], value)
        score_ref[k] = value / weight_ref[k]
    copies.append(pltpu.make_async_copy(score_ref, score_hbm, sems.at[chunks]))
    copies[-1].start()
    for copy in copies:
        copy.wait()


def spread_rows(own_terms, other_terms, ids, weights, select, scores, chunks):
    wide = own_terms[0].shape[1]
    width = wide - LANES
    tokens = select.shape[1]
    terms = len(own_terms)
    return pl.pallas_call(
        functools.partial(spread_kernel, chunks, terms),
        out_shape=[shape_of((tokens, width), jnp.bfloat16), shape_of(weights.shape, jnp.float32)],
        in_specs=[VMEM] * (2 * terms + 7),
        out_specs=[HBM, HBM],
        scratch_shapes=[
            pltpu.VMEM((tokens, width), jnp.bfloat16),
            pltpu.VMEM(weights.shape, jnp.float32),
            pltpu.SemaphoreType.DMA((chunks + 1,)),
        ],
        cost_estimate=cost(64 * tokens * width, 2 * tokens * width),
        compiler_params=pltpu.CompilerParams(vmem_limit_bytes=16 * 2**20),
        name="spread_rows",
    )(*own_terms, *other_terms, ids, weights, select, *scores)


def pairwise_shards(block_input, output_grad, expert_ids, gate_weights, gate_proj, up_proj, down_proj):
    tokens = block_input.shape[1]
    capacity = tokens // 16
    count = 2 * lax.axis_size("dp")
    plane = [offset for offset in range(count) if not offset & 2]
    offsets = plane + [offset | 2 for offset in plane]
    index = lax.axis_index(("dp", "expert")).astype(jnp.int32).reshape(1)
    ids = jnp.transpose(expert_ids, (2, 0, 1))
    weights = jnp.transpose(gate_weights, (2, 0, 1))
    stay = functools.partial(pltpu.with_memory_space_constraint, memory_space=pltpu.HBM)
    *sends, select, ids, weights = pick_rows(
        index, stay(ids), stay(weights), stay(block_input[0]), stay(output_grad[0]), capacity
    )
    gate, upper, lower = load_weights(*[stay(array[0, 0]) for array in (gate_proj, up_proj, down_proj)])
    mine = {0: sends[0]}
    for offset in sorted(plane[1:], reverse=True):
        mine[offset] = swap(sends[offset % 2], offset)
    theirs = {offset: swap(mine[offset], 2) for offset in plane}
    pieces = [mine[offset] for offset in plane] + [theirs[offset] for offset in plane]
    keep, send, delta, hidden, near, *far = hidden_pass(
        index, pieces, offsets, gate, upper, lower, capacity
    )
    recv = swap(send, 2)
    for scores in far:
        moved = swap(scores, 4)
        near = add_scores(near, moved)
    straight, crossed, *beyond = join_cores(keep, recv, capacity)
    own_terms, other_terms, grads = [], [], ()
    grads = weight_grads(is_first, pieces, delta, hidden, grads, 6)
    grads = weight_grads(is_last, pieces, delta, hidden, grads, 6)
    for rows in beyond:
        rows = send_back(rows, 1, 0)
        own_terms.append(rows)
        rows = lower_half(rows)
        other_terms.append(swap(rows, 2))
    own_terms.append(send_back(straight, 0, 0))
    other_terms.append(send_back(crossed, 0, 1))
    gate_grad, upper_grad, lower_grad = weight_grads(is_between, pieces, delta, hidden, grads, 6)
    scores = [near] + [swap(near, offset) for offset in (2, 1, 3)]
    received, weight_grad = spread_rows(own_terms, other_terms, ids, weights, select, scores, 3)
    return (
        received[None],
        jnp.transpose(weight_grad, (1, 2, 0)),
        gate_grad[None, None],
        upper_grad[None, None],
        lower_grad[None, None],
    )


def shifted(value, axis, steps):
    count = lax.axis_size(axis)
    pairs = [(source, (source + steps) % count) for source in range(count)]
    return lax.ppermute(value, axis, pairs)


def slot_tables(chosen_ids, experts, capacity):
    tok_count, chosen = chosen_ids.shape
    flat_ids = chosen_ids.reshape(-1)
    columns = jnp.arange(experts, dtype=jnp.int32)
    onehot = (flat_ids[:, None] == columns[None, :]).astype(jnp.int32)
    earlier = jnp.cumsum(onehot, axis=0) - onehot
    slot_rank = jnp.sum(earlier * onehot, axis=1)
    kept_pair = (flat_ids < experts) & (slot_rank < capacity)
    slot_index = jnp.where(kept_pair, flat_ids * capacity + slot_rank, experts * capacity)
    slot_rows = jnp.arange(experts * capacity, dtype=jnp.int32)
    placed = slot_index[None, :] == slot_rows[:, None]
    pair_index = jnp.arange(tok_count * chosen, dtype=jnp.int32)
    source_pair = jnp.sum(jnp.where(placed, pair_index[None, :], 0), axis=1)
    filled = jnp.any(placed, axis=1)
    return (slot_index, source_pair, filled)


def general_shards(block_input, output_grad, expert_ids, gate_weights, gate_proj, up_proj, down_proj):
    acts_local = block_input[0]
    grad_local = output_grad[0]
    chosen_ids = expert_ids[0]
    route_weight = gate_weights[0]
    tok_count, chosen = chosen_ids.shape
    width = acts_local.shape[1]
    local_count = gate_proj.shape[1]
    dp_count = lax.axis_size("dp")
    expert_count = lax.axis_size("expert")
    experts = local_count * expert_count
    capacity = tok_count // 16
    slot_index, source_pair, filled = slot_tables(chosen_ids, experts, capacity)
    source_token = source_pair // chosen
    slot_weight = route_weight.reshape(-1)[source_pair]
    send_acts = jnp.where(filled[:, None], acts_local[source_token], jnp.zeros((), jnp.bfloat16))
    scaled = slot_weight[:, None] * grad_local[source_token].astype(jnp.float32)
    send_grad = jnp.where(filled[:, None], scaled, 0.0).astype(jnp.bfloat16)
    send_acts = send_acts.reshape(experts, capacity, width)
    send_grad = send_grad.reshape(experts, capacity, width)
    acts_copies = jnp.broadcast_to(send_acts[None], (dp_count,) + send_acts.shape).reshape(
        dp_count * experts, capacity, width
    )
    grad_copies = jnp.broadcast_to(send_grad[None], (dp_count,) + send_grad.shape).reshape(
        dp_count * experts, capacity, width
    )
    recv_acts, recv_grad = (
        lax.all_to_all(acts_copies, ("dp", "expert"), split_axis=0, concat_axis=1, tiled=True),
        lax.all_to_all(grad_copies, ("dp", "expert"), split_axis=0, concat_axis=1, tiled=True),
    )
    gate_local = gate_proj[0]
    upper_local = up_proj[0]
    lower_local = down_proj[0]
    gate_pre = jnp.einsum("erd,edh->erh", recv_acts, gate_local, preferred_element_type=jnp.float32)
    up_value = jnp.einsum(
        "erd,edh->erh", recv_acts, upper_local, preferred_element_type=jnp.float32
    )
    grad_hidden = jnp.einsum(
        "erd,ehd->erh", recv_grad, lower_local, preferred_element_type=jnp.float32
    )
    sigma_gate = jax.nn.sigmoid(gate_pre)
    swish = gate_pre * sigma_gate
    hidden = swish * up_value
    scores = jnp.sum(hidden * grad_hidden, axis=2)
    lower_grad = jnp.einsum(
        "erh,erd->ehd", hidden.astype(jnp.bfloat16), recv_grad, preferred_element_type=jnp.float32
    ).astype(jnp.bfloat16)
    delta_gate = (
        grad_hidden * up_value * sigma_gate * (1.0 + gate_pre * (1.0 - sigma_gate))
    ).astype(jnp.bfloat16)
    delta_up = (grad_hidden * swish).astype(jnp.bfloat16)
    gate_grad = jnp.einsum(
        "erd,erh->edh", recv_acts, delta_gate, preferred_element_type=jnp.float32
    ).astype(jnp.bfloat16)
    upper_grad = jnp.einsum(
        "erd,erh->edh", recv_acts, delta_up, preferred_element_type=jnp.float32
    ).astype(jnp.bfloat16)
    partial_value = jnp.einsum(
        "erh,edh->erd", delta_gate, gate_local, preferred_element_type=jnp.float32
    ) + jnp.einsum("erh,edh->erd", delta_up, upper_local, preferred_element_type=jnp.float32)
    back_rows, back_scores = (
        lax.all_to_all(partial_value, ("dp", "expert"), split_axis=1, concat_axis=0, tiled=True),
        lax.all_to_all(scores, ("dp", "expert"), split_axis=1, concat_axis=0, tiled=True),
    )
    slot_grad = jnp.sum(back_rows.reshape(dp_count, experts * capacity, width), axis=0).astype(
        jnp.bfloat16
    )
    slot_scores = jnp.sum(back_scores.reshape(dp_count, experts * capacity), axis=0)
    token_rows = jnp.arange(tok_count, dtype=jnp.int32)
    token_map = ((source_token[:, None] == token_rows[None, :]) & filled[:, None]).astype(
        jnp.bfloat16
    )
    input_grad = jnp.einsum(
        "st,sd->td", token_map, slot_grad, preferred_element_type=jnp.float32
    ).astype(jnp.bfloat16)
    padded_scores = jnp.concatenate([slot_scores, jnp.zeros((1,), jnp.float32)])
    weight_grad = (padded_scores[slot_index] / route_weight.reshape(-1)).reshape(tok_count, chosen)
    received = shifted(input_grad, "pipe", -1)
    return (received[None], weight_grad[None], gate_grad[None], upper_grad[None], lower_grad[None])


def solution(mesh):
    in_specs = (
        P("pipe", ("dp", "expert"), None),
        P("pipe", ("dp", "expert"), None),
        P("pipe", ("dp", "expert"), None),
        P("pipe", ("dp", "expert"), None),
        P("pipe", "expert", None, "dp"),
        P("pipe", "expert", None, "dp"),
        P("pipe", "expert", "dp", None),
    )
    out_specs = (
        P("pipe", ("dp", "expert"), None),
        P("pipe", ("dp", "expert"), None),
        P("pipe", "expert", None, "dp"),
        P("pipe", "expert", None, "dp"),
        P("pipe", "expert", "dp", None),
    )
    dp_count, expert_count = mesh.shape["dp"], mesh.shape["expert"]

    def shards(*arrays):
        pairwise = (
            expert_count == 2
            and dp_count * expert_count <= PAIRWISE_MAX
            and dp_count > 1
            and power_of_two(dp_count)
            and arrays[4].shape[1] == 1
        )
        return (pairwise_shards if pairwise else general_shards)(*arrays)

    return jax.shard_map(shards, mesh=mesh, in_specs=in_specs, out_specs=out_specs, check_vma=False)
```

```python
import functools

import jax
import jax.numpy as jnp
from jax import lax
from jax.experimental import pallas as pl
from jax.experimental.pallas import tpu as pltpu
from jax.sharding import PartitionSpec as P


PAIRWISE_MAX = 8
EARLY = 3
LANES = 128
VMEM = pl.BlockSpec(memory_space=pltpu.VMEM)
HBM = pl.BlockSpec(memory_space=pltpu.HBM)


def shape_of(shape, dtype):
    return jax.ShapeDtypeStruct(shape, dtype)


def cost(flops, bytes_moved):
    return pl.CostEstimate(flops=flops, bytes_accessed=bytes_moved, transcendentals=0)


def power_of_two(number):
    return number > 0 and number & (number - 1) == 0


def swap(value, offset):
    count = lax.axis_size("dp") * lax.axis_size("expert")
    return lax.ppermute(value, ("dp", "expert"), [(i, i ^ offset) for i in range(count)])


def send_back(value, across, flip):
    sections = lax.axis_size("pipe")
    chips = lax.axis_size("dp") // 2
    pairs = []
    for s in range(sections):
        for x in range(chips):
            for core in range(2):
                for expert in range(2):
                    source = (s * chips + x) * 4 + 2 * core + expert
                    target = (((s - 1) % sections) * chips + (x ^ across)) * 4 + 2 * (expert ^ flip) + core
                    pairs.append((source, target))
    return lax.ppermute(value, ("pipe", "dp", "expert"), pairs)


def pick_kernel(capacity, index_ref, ids_hbm, weight_hbm, acts_hbm, grad_hbm, *refs):
    outs = refs[:2]
    select_ref, ids_ref, weight_ref, acts_ref, grad_ref, sems = refs[2:]
    copies = [
        pltpu.make_async_copy(source, target, sems.at[i])
        for i, (source, target) in enumerate(
            [(ids_hbm, ids_ref), (weight_hbm, weight_ref), (acts_hbm, acts_ref), (grad_hbm, grad_ref)]
        )
    ]
    for copy in copies:
        copy.start()
    chosen, _, tokens = ids_ref.shape
    width = acts_ref.shape[1]
    rows = 2 * capacity
    row = lax.broadcasted_iota(jnp.int32, (rows, tokens), 0)
    row_expert = (row // capacity) ^ (index_ref[0] & 1)
    before = lax.broadcasted_iota(jnp.int32, (tokens, tokens), 0)
    after = lax.broadcasted_iota(jnp.int32, (tokens, tokens), 1)
    earlier = jnp.where(before < after, 1.0, 0.0).astype(jnp.bfloat16)
    slot = (row % capacity).astype(jnp.float32)
    token = lax.broadcasted_iota(jnp.int32, (rows, tokens), 1).astype(jnp.float32)
    lane = lax.broadcasted_iota(jnp.int32, (rows, LANES), 1)
    taken = jnp.zeros((rows, tokens), jnp.float32)
    scale = jnp.zeros((rows, tokens), jnp.float32)
    copies[0].wait()
    copies[1].wait()
    for k in range(chosen):
        same = ids_ref[k] == row_expert
        taken = jnp.where(same, 1.0, taken)
        scale = jnp.where(same, weight_ref[k], scale)
    rank = jnp.dot(taken.astype(jnp.bfloat16), earlier, preferred_element_type=jnp.float32)
    select = jnp.where(rank == slot, taken, 0.0)
    row_scale = jnp.sum(select * scale, axis=1, keepdims=True)
    number = jnp.sum(select * (token + 1.0), axis=1, keepdims=True)
    high = jnp.floor(number / 256.0)
    marks = jnp.where(lane == 0, high, jnp.where(lane == 1, number - 256.0 * high, 0.0))
    select = select.astype(jnp.bfloat16)
    select_ref[...] = select
    copies[2].wait()
    acts_rows = jnp.dot(select, acts_ref[...], preferred_element_type=jnp.float32)
    copies[3].wait()
    grad_rows = jnp.dot(select, grad_ref[...], preferred_element_type=jnp.float32) * row_scale
    for j in range(2):
        part = slice(j * capacity, (j + 1) * capacity)
        outs[j][:, :width] = jnp.concatenate([acts_rows[part], grad_rows[part]], axis=0).astype(jnp.bfloat16)
        outs[j][:, width:] = jnp.concatenate([marks[part]] * 2, axis=0).astype(jnp.bfloat16)


def pick_rows(index, ids, weights, acts, grads, capacity):
    tokens, width = acts.shape
    group = shape_of((2 * capacity, width + LANES), jnp.bfloat16)
    return pl.pallas_call(
        functools.partial(pick_kernel, capacity),
        out_shape=[
            group,
            group,
            shape_of((2 * capacity, tokens), jnp.bfloat16),
            shape_of(ids.shape, jnp.int32),
            shape_of(weights.shape, jnp.float32),
        ],
        in_specs=[pl.BlockSpec(memory_space=pltpu.SMEM)] + [HBM] * 4,
        out_specs=[VMEM] * 5,
        scratch_shapes=[
            pltpu.VMEM((tokens, width), jnp.bfloat16),
            pltpu.VMEM((tokens, width), jnp.bfloat16),
            pltpu.SemaphoreType.DMA((4,)),
        ],
        cost_estimate=cost(8 * capacity * tokens * width, 4 * tokens * width),
        compiler_params=pltpu.CompilerParams(vmem_limit_bytes=16 * 2**20),
        name="pick_rows",
    )(index, ids, weights, acts, grads)


def load_kernel(*refs):
    count = len(refs) // 2
    sems = refs[-1]
    copies = [pltpu.make_async_copy(refs[i], refs[count + i], sems.at[i]) for i in range(count)]
    for copy in copies:
        copy.start()
    for copy in copies:
        copy.wait()


def load_weights(*arrays):
    return pl.pallas_call(
        load_kernel,
        out_shape=[shape_of(array.shape, array.dtype) for array in arrays],
        in_specs=[HBM] * len(arrays),
        out_specs=[VMEM] * len(arrays),
        scratch_shapes=[pltpu.SemaphoreType.DMA((len(arrays),))],
        cost_estimate=cost(0, 2 * sum(array.size for array in arrays)),
        compiler_params=pltpu.CompilerParams(vmem_limit_bytes=16 * 2**20),
        name="load_weights",
    )(*arrays)


def weave(value, capacity, upper):
    blank = jnp.zeros((capacity, value.shape[1]), value.dtype)
    parts = []
    for p in range(value.shape[0] // capacity):
        part = value[p * capacity : (p + 1) * capacity]
        parts += [part, blank] if upper else [blank, part]
    return jnp.concatenate(parts, axis=0)


def chain(steps):
    count = [0, 0]
    staged = []
    for unit, *_ in steps:
        staged.append(count[unit] % 2)
        count[unit] += 1
    ahead = 2
    for i in range(len(steps) + ahead):
        if i < len(steps):
            unit, weights, turned = steps[i][:3]
            pltpu.matmul_push_rhs(weights(), staging_register=staged[i], mxu_index=unit, transpose=turned)
        if i >= ahead:
            left, total, after = steps[i - ahead][3:]
            pltpu.matmul_acc_lhs(total, left(), load_staged_rhs=staged[i - ahead])
            if after is not None:
                after()


def hidden_kernel(capacity, offsets, index_ref, *refs):
    pieces = len(offsets)
    swapped = (index_ref[0] ^ (index_ref[0] >> 1)) & 1
    piece_refs = refs[:pieces]
    gate_ref, upper_ref, lower_ref = refs[pieces : pieces + 3]
    keep_ref, send_ref, delta_ref, hidden_ref = refs[pieces + 3 : pieces + 7]
    score_refs = refs[pieces + 7 :]
    width, units = gate_ref.shape
    rows = pieces * capacity
    half = rows // 2
    tile = units

    def acts(start):
        return jnp.concatenate([ref[:capacity, start : start + tile] for ref in piece_refs], axis=0)

    def grads(start):
        return jnp.concatenate([ref[capacity:, start : start + tile] for ref in piece_refs], axis=0)

    def order(value, wanted):
        lists = [
            jnp.concatenate(
                [value[offsets.index(o) * capacity : (offsets.index(o) + 1) * capacity] for o in chosen], axis=0
            )
            for chosen in wanted
        ]
        return jnp.where(swapped == 1, lists[1], lists[0])

    chips = [4 * x for x in range(pieces // 4)]
    kept = ([x | c for x in chips for c in (0, 2)], [x | c | 1 for x in chips for c in (2, 0)])
    sent = ([x | c | 1 for x in chips for c in (0, 2)], [x | c for x in chips for c in (2, 0)])

    def at(ref, start):
        return lambda: ref[start : start + tile]

    def at_column(ref, start):
        return lambda: ref[:, start : start + tile]

    def forward(first, second, third, fourth):
        taken = []

        def take():
            taken.extend((pltpu.matmul_pop(first), pltpu.matmul_pop(second)))

        steps = []
        for start in range(0, width, tile):
            left = functools.partial(acts, start)
            steps.append((0, at(gate_ref, start), False, left, first, None))
            steps.append((1, at(upper_ref, start), False, left, second, None))
        for i, start in enumerate(range(0, width, tile)):
            left = functools.partial(grads, start)
            total = (third, fourth)[i % 2]
            steps.append((i % 2, at_column(lower_ref, start), True, left, total, take if i == 1 else None))
        chain(steps)
        return (*taken, pltpu.matmul_pop(third) + pltpu.matmul_pop(fourth))

    totals = [pltpu.ACC(unit)((rows, tile), jnp.float32) for unit in range(2)]
    gate_pre, up_value, grad_hidden = pl.run_scoped(forward, *totals, *totals)
    sigma_gate = jax.nn.sigmoid(gate_pre)
    swish = gate_pre * sigma_gate
    hidden = swish * up_value
    scores = jnp.sum(hidden * grad_hidden, axis=1, keepdims=True)
    delta_gate = grad_hidden * up_value * sigma_gate * (1.0 + gate_pre * (1.0 - sigma_gate))
    delta_up = grad_hidden * swish
    marks = jnp.concatenate([ref[:, width:].astype(jnp.float32)[:capacity] for ref in piece_refs], axis=0)
    gate_part = jnp.concatenate([order(delta_gate, kept), order(delta_gate, sent)]).astype(jnp.bfloat16)
    upper_part = jnp.concatenate([order(delta_up, kept), order(delta_up, sent)]).astype(jnp.bfloat16)
    keep_ref[:, width:] = order(marks, kept)

    def back(*accs):
        starts = list(range(0, width, tile))

        def store(i):
            block = pltpu.matmul_pop(accs[i % len(accs)])
            keep_ref[:, starts[i] : starts[i] + tile] = block[:half]
            send_ref[:, starts[i] : starts[i] + tile] = block[half:].astype(jnp.bfloat16)

        steps = []
        for pair in range(0, len(starts), 2):
            for source in range(2):
                for i in range(pair, min(pair + 2, len(starts))):
                    weights = at((gate_ref, upper_ref)[source], starts[i])
                    left = (gate_part, upper_part)[source]
                    after = functools.partial(store, i - 2) if source == 0 and i >= 2 else None
                    steps.append((i % 2, weights, True, lambda left=left: left, accs[i % len(accs)], after))
        chain(steps)
        for i in range(max(0, len(starts) - 2), len(starts)):
            store(i)

    pl.run_scoped(back, *totals, *totals)
    lane = lax.broadcasted_iota(jnp.int32, (capacity, LANES), 1)
    for x, ref in enumerate(score_refs):
        spots = [offsets.index(4 * x + j) * capacity for j in range(4)]
        ref[...] = sum(jnp.where(lane == j, scores[spot : spot + capacity], 0.0) for j, spot in enumerate(spots))
    delta_ref[:, :units] = weave(delta_gate, capacity, True).astype(jnp.bfloat16)
    delta_ref[:, units:] = weave(delta_up, capacity, True).astype(jnp.bfloat16)
    hidden_ref[...] = weave(hidden, capacity, False).astype(jnp.bfloat16)


def hidden_pass(index, pieces, offsets, gate, upper, lower, capacity):
    width, units = gate.shape
    count = len(pieces)
    half = count * capacity // 2
    rows = 2 * count * capacity
    return pl.pallas_call(
        functools.partial(hidden_kernel, capacity, offsets),
        out_shape=[
            shape_of((half, width + LANES), jnp.float32),
            shape_of((half, width), jnp.bfloat16),
            shape_of((rows, 2 * units), jnp.bfloat16),
            shape_of((rows, units), jnp.bfloat16),
        ]
        + [shape_of((capacity, LANES), jnp.float32)] * (count // 4),
        in_specs=[pl.BlockSpec(memory_space=pltpu.SMEM)] + [VMEM] * (count + 3),
        out_specs=[VMEM] * (4 + count // 4),
        cost_estimate=cost(10 * rows * width * units, 6 * width * units),
        compiler_params=pltpu.CompilerParams(vmem_limit_bytes=24 * 2**20),
        name="hidden_pass",
    )(index, *pieces, gate, upper, lower)


def join_kernel(keep_ref, recv_ref, *out_refs):
    width = recv_ref.shape[1]
    start = 0
    for ref in out_refs:
        part = slice(start, start + ref.shape[0])
        ref[:, :width] = (keep_ref[part, :width] + recv_ref[part].astype(jnp.float32)).astype(jnp.bfloat16)
        if ref.shape[1] > width:
            ref[:, width:] = keep_ref[part, width:].astype(jnp.bfloat16)
        start += ref.shape[0]


def join_cores(keep, recv, capacity):
    half, wide = keep.shape
    far = half - 2 * capacity
    shapes = [(capacity, recv.shape[1] if far else wide)] * 2 + [(far, wide)] * (far > 0)
    return pl.pallas_call(
        join_kernel,
        out_shape=[shape_of(shape, jnp.bfloat16) for shape in shapes],
        in_specs=[VMEM] * 2,
        out_specs=[VMEM] * len(shapes),
        cost_estimate=cost(2 * half * wide, 8 * half * wide),
        compiler_params=pltpu.CompilerParams(vmem_limit_bytes=8 * 2**20),
        name="join_cores",
    )(keep, recv)


def weights_kernel(pieces, chunks, chosen, *refs):
    piece_refs = refs[:pieces]
    delta_ref, hidden_ref = refs[pieces : pieces + 2]
    hbm_refs, buffers, sems = refs[-7:-4], refs[-4:-1], refs[-1]
    width, units = buffers[0].shape
    down = (((0,), (0,)), ((), ()))

    def run(spots):
        copies = []
        for i in spots:
            part = slice(i * width // chunks, (i + 1) * width // chunks)
            rows = jnp.concatenate([ref[:, part] for ref in piece_refs], axis=0)
            both = lax.dot_general(rows, delta_ref[...], down, preferred_element_type=jnp.float32)
            buffers[0][part] = both[:, :units].astype(jnp.bfloat16)
            buffers[1][part] = both[:, units:].astype(jnp.bfloat16)
            buffers[2][:, part] = lax.dot_general(
                hidden_ref[...], rows, down, preferred_element_type=jnp.float32
            ).astype(jnp.bfloat16)
            for j, spot in enumerate(((part,), (part,), (slice(None), part))):
                copy = pltpu.make_async_copy(buffers[j].at[spot], hbm_refs[j].at[spot], sems.at[j, i])
                copy.start()
                copies.append(copy)
        for copy in copies:
            copy.wait()

    for predicate, spots in chosen:
        pl.when(predicate(lax.axis_index("pipe"), lax.axis_size("pipe")))(functools.partial(run, spots))


def weight_grads(chosen, pieces, delta, hidden, earlier, chunks):
    width = pieces[0].shape[1] - LANES
    rows, units = hidden.shape
    count = len(pieces)
    shapes = [(width, units), (width, units), (units, width)]
    return pl.pallas_call(
        functools.partial(weights_kernel, count, chunks, chosen),
        out_shape=[shape_of(shape, jnp.bfloat16) for shape in shapes],
        in_specs=[VMEM] * (count + 2) + [HBM] * len(earlier),
        out_specs=[HBM] * 3,
        input_output_aliases={2 + count + j: j for j in range(len(earlier))},
        scratch_shapes=[pltpu.VMEM(shape, jnp.bfloat16) for shape in shapes]
        + [pltpu.SemaphoreType.DMA((3, max(spots.stop for _, spots in chosen)))],
        cost_estimate=cost(6 * rows * width * units, 6 * width * units),
        compiler_params=pltpu.CompilerParams(vmem_limit_bytes=24 * 2**20),
        name="weight_grads",
    )(*pieces, delta, hidden, *earlier)


def is_first(section, sections):
    return section == 0


def is_last(section, sections):
    return (section == sections - 1) & (section != 0)


def is_between(section, sections):
    return (section != sections - 1) & (section != 0)


def cut_kernel(rows_ref, out_ref):
    out_ref[...] = rows_ref[out_ref.shape[0] :]


def lower_half(rows):
    count, wide = rows.shape
    return pl.pallas_call(
        cut_kernel,
        out_shape=shape_of((count // 2, wide), rows.dtype),
        in_specs=[VMEM],
        out_specs=VMEM,
        cost_estimate=cost(0, 4 * rows.size),
        compiler_params=pltpu.CompilerParams(vmem_limit_bytes=2 * 2**20),
        name="lower_half",
    )(rows)


def add_kernel(left_ref, right_ref, out_ref):
    out_ref[...] = left_ref[...] + right_ref[...]


def add_scores(left, right):
    return pl.pallas_call(
        add_kernel,
        out_shape=shape_of(left.shape, jnp.float32),
        in_specs=[VMEM] * 2,
        out_specs=VMEM,
        cost_estimate=cost(left.size, 12 * left.size),
        compiler_params=pltpu.CompilerParams(vmem_limit_bytes=2**20),
        name="add_scores",
    )(left, right)


def spread_kernel(chunks, terms, *refs):
    own_refs, other_refs = refs[:terms], refs[terms : 2 * terms]
    ids_ref, weight_ref, select_ref, near_ref, core_ref, side_ref, corner_ref = refs[2 * terms : 2 * terms + 7]
    out_hbm, score_hbm, out_ref, score_ref, sems = refs[2 * terms + 7 :]
    tokens, width = out_ref.shape
    capacity = other_refs[0].shape[0]
    marks = jnp.concatenate(
        [group[0][:capacity, width:].astype(jnp.float32) for group in (own_refs, other_refs)], axis=0
    )
    lane = lax.broadcasted_iota(jnp.int32, marks.shape, 1)
    number = jnp.sum(jnp.where(lane == 0, marks * 256.0, jnp.where(lane == 1, marks, 0.0)), axis=1, keepdims=True)
    token = lax.broadcasted_iota(jnp.int32, (2 * capacity, tokens), 1).astype(jnp.float32)
    select = jnp.where(token + 1.0 == number, 1.0, 0.0).astype(jnp.bfloat16)
    copies = []
    for i in range(chunks):
        part = slice(i * width // chunks, (i + 1) * width // chunks)
        rows = jnp.concatenate(
            [
                sum(ref[:capacity, part].astype(jnp.float32) for ref in group)
                for group in (own_refs, other_refs)
            ],
            axis=0,
        )
        out_ref[:, part] = lax.dot_general(
            select, rows.astype(jnp.bfloat16), (((0,), (0,)), ((), ())), preferred_element_type=jnp.float32
        ).astype(jnp.bfloat16)
        copies.append(pltpu.make_async_copy(out_ref.at[:, part], out_hbm.at[:, part], sems.at[i]))
        copies[-1].start()
    own = lax.axis_index("expert")
    scores = (near_ref[:, 0:1] + core_ref[:, 2:3], side_ref[:, 1:2] + corner_ref[:, 3:4])
    sums = []
    for j in range(2):
        picked = select_ref[j * capacity : (j + 1) * capacity].astype(jnp.float32) * scores[j]
        sums.append(jnp.sum(picked, axis=0, keepdims=True))
    for k in range(ids_ref.shape[0]):
        value = jnp.zeros((1, tokens), jnp.float32)
        for j in range(2):
            value = jnp.where(ids_ref[k] == (own ^ j), sums[j], value)
        score_ref[k] = value / weight_ref[k]
    copies.append(pltpu.make_async_copy(score_ref, score_hbm, sems.at[chunks]))
    copies[-1].start()
    for copy in copies:
        copy.wait()


def spread_rows(own_terms, other_terms, ids, weights, select, scores, chunks):
    wide = own_terms[0].shape[1]
    width = wide - LANES
    tokens = select.shape[1]
    terms = len(own_terms)
    return pl.pallas_call(
        functools.partial(spread_kernel, chunks, terms),
        out_shape=[shape_of((tokens, width), jnp.bfloat16), shape_of(weights.shape, jnp.float32)],
        in_specs=[VMEM] * (2 * terms + 7),
        out_specs=[HBM, HBM],
        scratch_shapes=[
            pltpu.VMEM((tokens, width), jnp.bfloat16),
            pltpu.VMEM(weights.shape, jnp.float32),
            pltpu.SemaphoreType.DMA((chunks + 1,)),
        ],
        cost_estimate=cost(64 * tokens * width, 2 * tokens * width),
        compiler_params=pltpu.CompilerParams(vmem_limit_bytes=16 * 2**20),
        name="spread_rows",
    )(*own_terms, *other_terms, ids, weights, select, *scores)


def pairwise_shards(block_input, output_grad, expert_ids, gate_weights, gate_proj, up_proj, down_proj):
    tokens = block_input.shape[1]
    capacity = tokens // 16
    count = 2 * lax.axis_size("dp")
    plane = [offset for offset in range(count) if not offset & 2]
    offsets = plane + [offset | 2 for offset in plane]
    index = lax.axis_index(("dp", "expert")).astype(jnp.int32).reshape(1)
    ids = jnp.transpose(expert_ids, (2, 0, 1))
    weights = jnp.transpose(gate_weights, (2, 0, 1))
    stay = functools.partial(pltpu.with_memory_space_constraint, memory_space=pltpu.HBM)
    *sends, select, ids, weights = pick_rows(
        index, stay(ids), stay(weights), stay(block_input[0]), stay(output_grad[0]), capacity
    )
    gate, upper, lower = load_weights(*[stay(array[0, 0]) for array in (gate_proj, up_proj, down_proj)])
    mine = {0: sends[0]}
    for offset in sorted(plane[1:], reverse=True):
        mine[offset] = swap(sends[offset % 2], offset)
    theirs = {offset: swap(mine[offset], 2) for offset in plane}
    pieces = [mine[offset] for offset in plane] + [theirs[offset] for offset in plane]
    keep, send, delta, hidden, near, *far = hidden_pass(
        index, pieces, offsets, gate, upper, lower, capacity
    )
    recv = swap(send, 2)
    for scores in far:
        moved = swap(scores, 4)
        near = add_scores(near, moved)
    straight, crossed, *beyond = join_cores(keep, recv, capacity)
    own_terms, other_terms, grads = [], [], ()
    grads = weight_grads([(is_first, range(EARLY))], pieces, delta, hidden, grads, 6)
    grads = weight_grads([(is_last, range(3))], pieces, delta, hidden, grads, 3)
    for rows in beyond:
        rows = send_back(rows, 1, 0)
        own_terms.append(rows)
        rows = lower_half(rows)
        other_terms.append(swap(rows, 2))
    own_terms.append(send_back(straight, 0, 0))
    other_terms.append(send_back(crossed, 0, 1))
    gate_grad, upper_grad, lower_grad = weight_grads(
        [(is_first, range(EARLY, 6)), (is_between, range(6))], pieces, delta, hidden, grads, 6
    )
    scores = [near] + [swap(near, offset) for offset in (2, 1, 3)]
    received, weight_grad = spread_rows(own_terms, other_terms, ids, weights, select, scores, 3)
    return (
        received[None],
        jnp.transpose(weight_grad, (1, 2, 0)),
        gate_grad[None, None],
        upper_grad[None, None],
        lower_grad[None, None],
    )


def shifted(value, axis, steps):
    count = lax.axis_size(axis)
    pairs = [(source, (source + steps) % count) for source in range(count)]
    return lax.ppermute(value, axis, pairs)


def slot_tables(chosen_ids, experts, capacity):
    tok_count, chosen = chosen_ids.shape
    flat_ids = chosen_ids.reshape(-1)
    columns = jnp.arange(experts, dtype=jnp.int32)
    onehot = (flat_ids[:, None] == columns[None, :]).astype(jnp.int32)
    earlier = jnp.cumsum(onehot, axis=0) - onehot
    slot_rank = jnp.sum(earlier * onehot, axis=1)
    kept_pair = (flat_ids < experts) & (slot_rank < capacity)
    slot_index = jnp.where(kept_pair, flat_ids * capacity + slot_rank, experts * capacity)
    slot_rows = jnp.arange(experts * capacity, dtype=jnp.int32)
    placed = slot_index[None, :] == slot_rows[:, None]
    pair_index = jnp.arange(tok_count * chosen, dtype=jnp.int32)
    source_pair = jnp.sum(jnp.where(placed, pair_index[None, :], 0), axis=1)
    filled = jnp.any(placed, axis=1)
    return (slot_index, source_pair, filled)


def general_shards(block_input, output_grad, expert_ids, gate_weights, gate_proj, up_proj, down_proj):
    acts_local = block_input[0]
    grad_local = output_grad[0]
    chosen_ids = expert_ids[0]
    route_weight = gate_weights[0]
    tok_count, chosen = chosen_ids.shape
    width = acts_local.shape[1]
    local_count = gate_proj.shape[1]
    dp_count = lax.axis_size("dp")
    expert_count = lax.axis_size("expert")
    experts = local_count * expert_count
    capacity = tok_count // 16
    slot_index, source_pair, filled = slot_tables(chosen_ids, experts, capacity)
    source_token = source_pair // chosen
    slot_weight = route_weight.reshape(-1)[source_pair]
    send_acts = jnp.where(filled[:, None], acts_local[source_token], jnp.zeros((), jnp.bfloat16))
    scaled = slot_weight[:, None] * grad_local[source_token].astype(jnp.float32)
    send_grad = jnp.where(filled[:, None], scaled, 0.0).astype(jnp.bfloat16)
    send_acts = send_acts.reshape(experts, capacity, width)
    send_grad = send_grad.reshape(experts, capacity, width)
    acts_copies = jnp.broadcast_to(send_acts[None], (dp_count,) + send_acts.shape).reshape(
        dp_count * experts, capacity, width
    )
    grad_copies = jnp.broadcast_to(send_grad[None], (dp_count,) + send_grad.shape).reshape(
        dp_count * experts, capacity, width
    )
    recv_acts, recv_grad = (
        lax.all_to_all(acts_copies, ("dp", "expert"), split_axis=0, concat_axis=1, tiled=True),
        lax.all_to_all(grad_copies, ("dp", "expert"), split_axis=0, concat_axis=1, tiled=True),
    )
    gate_local = gate_proj[0]
    upper_local = up_proj[0]
    lower_local = down_proj[0]
    gate_pre = jnp.einsum("erd,edh->erh", recv_acts, gate_local, preferred_element_type=jnp.float32)
    up_value = jnp.einsum(
        "erd,edh->erh", recv_acts, upper_local, preferred_element_type=jnp.float32
    )
    grad_hidden = jnp.einsum(
        "erd,ehd->erh", recv_grad, lower_local, preferred_element_type=jnp.float32
    )
    sigma_gate = jax.nn.sigmoid(gate_pre)
    swish = gate_pre * sigma_gate
    hidden = swish * up_value
    scores = jnp.sum(hidden * grad_hidden, axis=2)
    lower_grad = jnp.einsum(
        "erh,erd->ehd", hidden.astype(jnp.bfloat16), recv_grad, preferred_element_type=jnp.float32
    ).astype(jnp.bfloat16)
    delta_gate = (
        grad_hidden * up_value * sigma_gate * (1.0 + gate_pre * (1.0 - sigma_gate))
    ).astype(jnp.bfloat16)
    delta_up = (grad_hidden * swish).astype(jnp.bfloat16)
    gate_grad = jnp.einsum(
        "erd,erh->edh", recv_acts, delta_gate, preferred_element_type=jnp.float32
    ).astype(jnp.bfloat16)
    upper_grad = jnp.einsum(
        "erd,erh->edh", recv_acts, delta_up, preferred_element_type=jnp.float32
    ).astype(jnp.bfloat16)
    partial_value = jnp.einsum(
        "erh,edh->erd", delta_gate, gate_local, preferred_element_type=jnp.float32
    ) + jnp.einsum("erh,edh->erd", delta_up, upper_local, preferred_element_type=jnp.float32)
    back_rows, back_scores = (
        lax.all_to_all(partial_value, ("dp", "expert"), split_axis=1, concat_axis=0, tiled=True),
        lax.all_to_all(scores, ("dp", "expert"), split_axis=1, concat_axis=0, tiled=True),
    )
    slot_grad = jnp.sum(back_rows.reshape(dp_count, experts * capacity, width), axis=0).astype(
        jnp.bfloat16
    )
    slot_scores = jnp.sum(back_scores.reshape(dp_count, experts * capacity), axis=0)
    token_rows = jnp.arange(tok_count, dtype=jnp.int32)
    token_map = ((source_token[:, None] == token_rows[None, :]) & filled[:, None]).astype(
        jnp.bfloat16
    )
    input_grad = jnp.einsum(
        "st,sd->td", token_map, slot_grad, preferred_element_type=jnp.float32
    ).astype(jnp.bfloat16)
    padded_scores = jnp.concatenate([slot_scores, jnp.zeros((1,), jnp.float32)])
    weight_grad = (padded_scores[slot_index] / route_weight.reshape(-1)).reshape(tok_count, chosen)
    received = shifted(input_grad, "pipe", -1)
    return (received[None], weight_grad[None], gate_grad[None], upper_grad[None], lower_grad[None])


def solution(mesh):
    in_specs = (
        P("pipe", ("dp", "expert"), None),
        P("pipe", ("dp", "expert"), None),
        P("pipe", ("dp", "expert"), None),
        P("pipe", ("dp", "expert"), None),
        P("pipe", "expert", None, "dp"),
        P("pipe", "expert", None, "dp"),
        P("pipe", "expert", "dp", None),
    )
    out_specs = (
        P("pipe", ("dp", "expert"), None),
        P("pipe", ("dp", "expert"), None),
        P("pipe", "expert", None, "dp"),
        P("pipe", "expert", None, "dp"),
        P("pipe", "expert", "dp", None),
    )
    dp_count, expert_count = mesh.shape["dp"], mesh.shape["expert"]

    def shards(*arrays):
        pairwise = (
            expert_count == 2
            and dp_count * expert_count <= PAIRWISE_MAX
            and dp_count > 1
            and power_of_two(dp_count)
            and arrays[4].shape[1] == 1
        )
        return (pairwise_shards if pairwise else general_shards)(*arrays)

    return jax.shard_map(shards, mesh=mesh, in_specs=in_specs, out_specs=out_specs, check_vma=False)
```
